32 devices in a mesh: clip: 2 (over x), blk: 16 (over z, y, core).
Axes of the slice: x: 2, y: 2, z: 4, core: 2. Of those that a mesh axis runs over, the one named last changes fastest.
Arguments:
- queries: bfloat16 [8192, 2560], P(('clip', 'blk')), parts along dimension 0, may hold values from -24 to 24
- keys: bfloat16 [8192, 2560], P(('clip', 'blk')), parts along dimension 0, may hold values from -24 to 24
- values: bfloat16 [8192, 2560], P(('clip', 'blk')), parts along dimension 0, may hold values from -6 to 6
- kept_blocks: int32 [64, 8], P(('clip', 'blk')), parts along dimension 0, may hold values from 0 to 31, as said below
Outputs:
- attended: bfloat16 [8192, 2560], P(('clip', 'blk')), parts along dimension 0
The draws below stay inside these ranges and needn't reach their ends.
There are 2 independent parts, one for each index of `clip`. The reference program is written for one: setup_inputs(seed, part) draws one part's arguments, and reference() takes and returns one part's arrays. A program takes and returns all parts, laid end to end along the dimension named above; each array names one. Nothing has to cross between parts.
Inputs may be any that keep to these rules, and one draw needn't show every extreme that they name: `kept_blocks`: row b lists 8 distinct key blocks in increasing order; b itself is one of them, and for every listed block j the difference j // 2 - b // 2 is 0 or plus or minus a power of two of at most 8.
All inputs are finite; a program needn't handle non-finite values.
Results may differ from the reference program's by a relative error of at most 0.0065.
Values may be sent and summed in bfloat16 or wider, within the bound.
A program may use at most 128 MiB of HBM per device.

```python
import math
import jax
import jax.numpy as jnp
from jax import lax

H = 20
DH = 128
BLOCK = 128
BD = 2
KEEP = 8
REACH = 8
NB = 32
SEQ = 4096


def draw_queries(key, part):
    values_drawn = jnp.clip(jax.random.normal(jax.random.fold_in(key, 1), (SEQ, H * DH), jnp.float32), -4.0, 4.0)
    return values_drawn.astype(jnp.bfloat16)


def draw_keys(key, part):
    values_drawn = jnp.clip(jax.random.normal(jax.random.fold_in(key, 2), (SEQ, H * DH), jnp.float32), -4.0, 4.0)
    return values_drawn.astype(jnp.bfloat16)


def draw_kept_blocks(key, part):
    blocks = jnp.arange(NB, dtype=jnp.int32)
    owner_device = blocks // BD
    offsets = [0]
    distance = 1
    farthest = min(REACH, NB // BD - 1)
    while distance <= farthest:
        offsets = offsets + [distance, -distance]
        distance = distance * 2
    columns = []
    for offset in offsets:
        for within in range(BD):
            columns.append((owner_device + offset) * BD + within)
    candidates = jnp.stack(columns, axis=1).astype(jnp.int32)
    candidate_count = candidates.shape[1]
    usable = (candidates >= 0) & (candidates < NB) & (candidates != blocks[:, None])
    random_rank = jax.random.randint(jax.random.fold_in(key, 7), (NB, candidate_count), 0, 4096, dtype=jnp.int32)
    ranking = jnp.where(usable, random_rank * candidate_count + jnp.arange(candidate_count, dtype=jnp.int32)[None, :], -1)
    ranked, picked = lax.top_k(ranking, KEEP - 1)
    chosen = jnp.take_along_axis(candidates, picked, axis=1)
    return jnp.sort(jnp.concatenate([blocks[:, None], chosen], axis=1), axis=1).astype(jnp.int32)


def shard_levels(rng, extent, shards, low, largest):
    loudness = 1.0
    for dim, blocks in shards:
        steps = jax.random.uniform(jax.random.fold_in(jax.random.fold_in(rng, 6), dim), (blocks,), jnp.float32, low / len(shards), largest / len(shards))
        loudness = loudness * jnp.repeat(jnp.exp(steps), extent[dim] // blocks).reshape((-1,) + (1,) * (len(extent) - 1 - dim))
    return loudness


def scatter_about(rng, dims, spread, bound, shards=(), held_as=jnp.bfloat16):
    array = spread * jax.random.normal(rng, dims, jnp.float32)
    if shards:
        array = array * shard_levels(rng, dims, shards, -0.22, 0.18)
    return jnp.clip(array, -bound, bound).astype(held_as)


def setup_inputs(seed: int = 0, part: int = 0) -> dict:
    key_list = jax.random.split(jax.random.key(seed), 5)
    part_splits = jax.random.split(jax.random.fold_in(key_list[4], part), 5)
    queries = draw_queries(jax.random.fold_in(jax.random.fold_in(key_list[4], part), 71), part)
    keys = draw_keys(jax.random.fold_in(jax.random.fold_in(key_list[4], part), 71), part)
    values = scatter_about(part_splits[2], (SEQ, H * DH), 1.0, 6.0, ((0, 16),))
    kept_blocks = draw_kept_blocks(jax.random.fold_in(jax.random.fold_in(key_list[4], part), 71), part)
    return dict(queries=queries, keys=keys, values=values, kept_blocks=kept_blocks)


def reference(queries, keys, values, kept_blocks):
    query_all = queries.reshape(NB, BLOCK, H, DH)
    key_all = keys.reshape(NB, BLOCK, H, DH)
    value_all = values.reshape(NB, BLOCK, H, DH)
    scale_factor = 1.0 / math.sqrt(DH)

    def attend_block(block_number):
        listed = kept_blocks[block_number].astype(jnp.int32)
        query_rows = query_all[block_number].astype(jnp.float32)
        key_rows = key_all[listed].reshape(KEEP * BLOCK, H, DH).astype(jnp.float32)
        value_rows = value_all[listed].reshape(KEEP * BLOCK, H, DH).astype(jnp.float32)
        scores = jnp.einsum('qhd,khd->hqk', query_rows, key_rows) * scale_factor
        top = lax.optimization_barrier(jnp.max(scores, axis=-1))
        weight = jnp.exp(scores - top[..., None])
        total = lax.optimization_barrier(jnp.sum(weight, axis=-1))
        rounded = lax.optimization_barrier(weight.astype(jnp.bfloat16)).astype(jnp.float32)
        numerator = jnp.einsum('hqk,khd->qhd', rounded, value_rows)
        result = numerator / jnp.transpose(total)[:, :, None]
        return result.astype(jnp.bfloat16)
    outputs = lax.map(attend_block, jnp.arange(NB, dtype=jnp.int32))
    return outputs.reshape(SEQ, H * DH)
```

```python
import functools
import math

import jax
import jax.numpy as jnp
from jax import lax
from jax.experimental import pallas as pl
from jax.experimental.pallas import tpu as pltpu
from jax.sharding import PartitionSpec as P

DH = 128
BLOCK = 128

OFFSETS = (1, -1, 2, -2, 4, -4, 8, -8, 0)
OWN = 8
MASKED = -1e30
C_EXP = math.log2(math.e) / math.sqrt(DH)


def kernel(
    n, heads, kept_hbm, q_hbm, k_hbm, v_hbm, out_ref,
    kv, kept_ref, q_vmem, scores, bias, local_sem, kept_sem, q_sem, send_sem, recv_sem,
):
    rows = kv.shape[-2]
    local_blocks = rows // BLOCK
    d = lax.axis_index("blk")
    r = lax.rem(d, 4)
    upper = r // 2
    odd = lax.rem(r, 2)
    straight = odd == upper
    crossed = odd != upper

    pair = d + 2 - 4 * upper
    mate = d + 1 - 2 * odd
    has_up = d + 4 < n
    has_down = d - 4 >= 0
    both = jnp.logical_and(has_up, has_down)

    held = heads // 2
    lag = held + 1

    def columns(h):
        return pl.ds(pl.multiple_of(h * DH, DH), DH)

    def local_copies(h):
        return [
            pltpu.make_async_copy(hbm.at[:, columns(h)], kv.at[OWN, h, i], local_sem.at[i, h])
            for i, hbm in ((0, k_hbm), (1, v_hbm))
        ]

    def flow(index, src_slot, dst_slot, target, h):
        return pltpu.make_async_remote_copy(
            src_ref=kv.at[src_slot, h],
            dst_ref=kv.at[dst_slot, h],
            send_sem=send_sem.at[index],
            recv_sem=recv_sem.at[dst_slot, h],
            device_id={"blk": target},
            device_id_type=pl.DeviceIdType.MESH,
        )

    def received(slot, sender, h):
        return pltpu.make_async_remote_copy(
            src_ref=kv.at[slot, h],
            dst_ref=kv.at[slot, h],
            send_sem=send_sem.at[0],
            recv_sem=recv_sem.at[slot, h],
            device_id={"blk": sender},
            device_id_type=pl.DeviceIdType.MESH,
        )

    def sent(index, src_slot, target):
        return pltpu.make_async_remote_copy(
            src_ref=kv.at[src_slot],
            dst_ref=kv.at[src_slot],
            send_sem=send_sem.at[index],
            recv_sem=recv_sem.at[src_slot, 0],
            device_id={"blk": target},
            device_id_type=pl.DeviceIdType.MESH,
        )

    own_up = (0, OWN, 5, d + 4, has_up)
    own_down = (1, OWN, 4, d - 4, has_down)
    own_pair = (2, OWN, 3 - upper, pair, None)
    own_mate = (3, OWN, 1 - odd, mate, None)
    pass_flows = (
        (4, 5, 7, d + 4, both),
        (5, 4, 6, d - 4, both),
        (6, 4 + upper, 2 + upper, pair, jnp.where(upper == 1, d - 4 >= 0, d + 4 < n)),
    )
    hand_on = (7, 2 + odd, odd, mate, jnp.where(odd == 1, d - 2 >= 0, d + 2 < n))

    def when(condition, action):
        if condition is None:
            action()
        else:
            pl.when(condition)(action)

    def start(flows, h):
        for index, src, dst, target, condition in flows:
            when(condition, lambda: flow(index, src, dst, target, h).start())

    def arrive(slot, sender, condition, h):
        when(condition, lambda: received(slot, sender, h).wait_recv())

    @pl.loop(0, heads)
    def _(h):
        for c in local_copies(h):
            c.start()

    barrier = pltpu.get_barrier_semaphore()
    for target, condition in ((d + 4, has_up), (d - 4, has_down), (pair, None), (mate, None)):
        when(
            condition,
            lambda: pl.semaphore_signal(
                barrier, inc=1, device_id={"blk": target}, device_id_type=pl.DeviceIdType.MESH
            ),
        )
    q_copy = pltpu.make_async_copy(q_hbm, q_vmem, q_sem)
    q_copy.start()
    kept_copy = pltpu.make_async_copy(kept_hbm, kept_ref, kept_sem)
    kept_copy.start()
    pl.semaphore_wait(barrier, 2 + has_up.astype(jnp.int32) + has_down.astype(jnp.int32))

    @pl.loop(0, heads)
    def _(h):
        for c in local_copies(h):
            c.wait()
        start((own_up, own_down), h)

        @pl.when(jnp.logical_or(crossed, h < held))
        def _():
            start((own_pair,), h)

        start((own_mate,), h)

    for slot, offset in enumerate(OFFSETS[:OWN]):
        source = d + offset

        @pl.when(jnp.logical_or(source < 0, source >= n))
        def _():
            @pl.loop(0, heads)
            def _(h):
                kv[slot, h] = jnp.zeros(kv.shape[2:], kv.dtype)

    def prepare():
        kept_copy.wait()
        for query_slot in range(local_blocks):
            kept = [kept_ref[query_slot, j] for j in range(kept_ref.shape[1])]
            for slot, offset in enumerate(OFFSETS):
                inside = jnp.logical_and(d + offset >= 0, d + offset < n)
                for key_slot in range(local_blocks):
                    block = (d + offset) * local_blocks + key_slot
                    allowed = functools.reduce(jnp.logical_or, [j == block for j in kept])
                    bias[slot, pl.ds(query_slot, 1), pl.ds(key_slot * BLOCK, BLOCK)] = jnp.full(
                        (1, BLOCK), jnp.where(jnp.logical_and(allowed, inside), 0.0, MASKED), jnp.float32
                    )
        q_copy.wait()

    prepare()

    def hand_over(h):
        arrive(2 + odd, pair, hand_on[-1], h)
        start((hand_on,), h)

    @pl.loop(0, heads)
    def _(h):
        arrive(5, d - 4, has_down, h)
        arrive(4, d + 4, has_up, h)
        start(pass_flows, h)

        @pl.when(straight)
        def _():
            hand_over(h)

        @pl.when(jnp.logical_and(crossed, h >= lag))
        def _():
            hand_over(h - lag)

    @pl.when(straight)
    def _():
        @pl.loop(held, heads)
        def _(h):
            start((own_pair,), h)

    def part(q, h, slots):
        tops = [None] * local_blocks
        for i, slot in enumerate(slots):
            s = lax.dot_general(
                q, kv[slot, h, 0], (((1,), (1,)), ((), ())), preferred_element_type=jnp.float32
            )
            for b in range(local_blocks):
                masked = s[b * BLOCK : (b + 1) * BLOCK] + bias[slot, b : b + 1, :]
                scores[i, b * BLOCK : (b + 1) * BLOCK] = masked
                tops[b] = masked if tops[b] is None else jnp.maximum(tops[b], masked)
        return jnp.concatenate([jnp.max(t, axis=1, keepdims=True) for t in tops], axis=0)

    def weigh(h, slots, top):
        sums = None
        numerator = None
        for i, slot in enumerate(slots):
            weight = jnp.exp2((scores[i] - top) * C_EXP)
            sums = weight if sums is None else sums + weight
            term = jnp.dot(
                weight.astype(jnp.bfloat16), kv[slot, h, 1], preferred_element_type=jnp.float32
            )
            numerator = term if numerator is None else numerator + term
        return jnp.sum(sums, axis=1, keepdims=True), numerator

    early = (OWN, 4, 5, 0, 1, 2 + odd)
    late = (3 - odd, 6, 7)

    @pl.loop(0, heads)
    def _(h):
        @pl.when(jnp.logical_and(crossed, h + heads - lag < heads))
        def _():
            hand_over(h + heads - lag)

        q = q_vmem[:, columns(h)]
        arrive(odd, mate, None, h)
        arrive(1 - odd, mate, jnp.where(odd == 1, d + 1 < n, d - 1 >= 0), h)
        top_early = part(q, h, early)
        total_early, numerator_early = weigh(h, early, top_early)

        arrive(3 - odd, pair, jnp.where(odd == 1, d + 2 < n, d - 2 >= 0), h)
        arrive(7, d - 4, d - 8 >= 0, h)
        arrive(6, d + 4, d + 8 < n, h)
        top = jnp.maximum(top_early, part(q, h, late))
        total, numerator = weigh(h, late, top)
        shrink = jnp.exp2((top_early - top) * C_EXP)
        total = total + total_early * shrink
        out_ref[:, columns(h)] = ((numerator + numerator_early * shrink) / total).astype(out_ref.dtype)

    for index, src, dst, target, condition in (own_up, own_down, own_pair, own_mate, *pass_flows, hand_on):
        when(condition, lambda: sent(index, src, target).wait_send())


def per_device(queries, keys, values, kept_blocks):
    n = lax.axis_size("blk")
    rows, features = queries.shape
    heads = features // DH
    slots = len(OFFSETS)
    inputs = [
        pltpu.with_memory_space_constraint(x, pltpu.HBM) for x in (kept_blocks, queries, keys, values)
    ]
    return pl.pallas_call(
        functools.partial(kernel, n, heads),
        out_shape=jax.ShapeDtypeStruct((rows, features), jnp.bfloat16),
        in_specs=[pl.BlockSpec(memory_space=pltpu.HBM)] * 4,
        out_specs=pl.BlockSpec(memory_space=pltpu.VMEM),
        scratch_shapes=[
            pltpu.VMEM((slots, heads, 2, rows, DH), jnp.bfloat16),
            pltpu.SMEM(kept_blocks.shape, jnp.int32),
            pltpu.VMEM((rows, features), jnp.bfloat16),
            pltpu.VMEM((6, rows, rows), jnp.float32),
            pltpu.VMEM((slots, rows // BLOCK, rows), jnp.float32),
            pltpu.SemaphoreType.DMA((2, heads)),
            pltpu.SemaphoreType.DMA,
            pltpu.SemaphoreType.DMA,
            pltpu.SemaphoreType.DMA((8,)),
            pltpu.SemaphoreType.DMA((8, heads)),
        ],
        compiler_params=pltpu.CompilerParams(
            collective_id=0, has_side_effects=True, vmem_limit_bytes=40 * 2**20
        ),
    )(*inputs)


def solution(mesh):
    placed = P(("clip", "blk"), None)
    return jax.shard_map(
        per_device, mesh=mesh, in_specs=(placed,) * 4, out_specs=placed, check_vma=False
    )
```

```python
import functools
import math

import jax
import jax.numpy as jnp
from jax import lax
from jax.experimental import pallas as pl
from jax.experimental.pallas import tpu as pltpu
from jax.sharding import PartitionSpec as P

DH = 128
BLOCK = 128
AHEAD = 4
LENT = 6
FIRST = 2

OFFSETS = (1, -1, 2, -2, 4, -4, 8, -8, 0)
OWN = 8
MASKED = -1e30
C_EXP = math.log2(math.e) / math.sqrt(DH)


def kernel(
    n, heads, lent, kept_hbm, q_hbm, k_hbm, v_hbm, out_ref,
    kv, kept_ref, q_vmem, scores, bias, guest_q, guest_bias, back, back_stats, given, given_stats,
    local_sem, kept_sem, q_sem, send_sem, recv_sem, lend_send, lend_recv, back_recv,
):
    rows = kv.shape[-2]
    local_blocks = rows // BLOCK
    d = lax.axis_index("blk")
    r = lax.rem(d, 4)
    upper = r // 2
    odd = lax.rem(r, 2)
    straight = odd == upper
    crossed = odd != upper

    pair = d + 2 - 4 * upper
    mate = d + 1 - 2 * odd
    has_up = d + 4 < n
    has_down = d - 4 >= 0
    both = jnp.logical_and(has_up, has_down)

    low, high = d < 4, d + 4 >= n
    serves_low = jnp.logical_and(d >= 4, d < 8)
    serves_high = jnp.logical_and(d + 4 < n, d + 8 >= n)
    lends = jnp.logical_or(low, high)
    serves = jnp.logical_or(serves_low, serves_high)
    server = jnp.where(low, d + 4, d - 4)
    guest = jnp.where(serves_low, d - 4, d + 4)
    missing = jnp.where(low, 6, 7)
    served = jnp.where(serves_low, 4, 5)

    held = heads // 2
    lag = held + 1

    def columns(h):
        return pl.ds(pl.multiple_of(h * DH, DH), DH)

    def local_copies(h):
        return [
            pltpu.make_async_copy(hbm.at[:, columns(h)], kv.at[OWN, h, i], local_sem.at[i, h])
            for i, hbm in ((0, k_hbm), (1, v_hbm))
        ]

    def flow(index, src_slot, dst_slot, target, h):
        return pltpu.make_async_remote_copy(
            src_ref=kv.at[src_slot, h],
            dst_ref=kv.at[dst_slot, h],
            send_sem=send_sem.at[index],
            recv_sem=recv_sem.at[dst_slot, h],
            device_id={"blk": target},
            device_id_type=pl.DeviceIdType.MESH,
        )

    def received(slot, sender, h):
        return pltpu.make_async_remote_copy(
            src_ref=kv.at[slot, h],
            dst_ref=kv.at[slot, h],
            send_sem=send_sem.at[0],
            recv_sem=recv_sem.at[slot, h],
            device_id={"blk": sender},
            device_id_type=pl.DeviceIdType.MESH,
        )

    def sent(index, src_slot, target, skipped):
        some = pl.ds(skipped, heads - skipped)
        return pltpu.make_async_remote_copy(
            src_ref=kv.at[src_slot, some],
            dst_ref=kv.at[src_slot, some],
            send_sem=send_sem.at[index],
            recv_sem=recv_sem.at[src_slot, 0],
            device_id={"blk": target},
            device_id_type=pl.DeviceIdType.MESH,
        )

    own_up = (0, OWN, 5, d + 4, has_up)
    own_down = (1, OWN, 4, d - 4, has_down)
    own_pair = (2, OWN, 3 - upper, pair, None)
    own_mate = (3, OWN, 1 - odd, mate, None)
    pass_flows = (
        (4, 5, 7, d + 4, both),
        (5, 4, 6, d - 4, both),
        (6, 4 + upper, 2 + upper, pair, jnp.where(upper == 1, d - 4 >= 0, d + 4 < n)),
    )
    hand_on = (7, 2 + odd, odd, mate, jnp.where(odd == 1, d - 2 >= 0, d + 2 < n))

    def remote(src, dst, sends, receives, target):
        return pltpu.make_async_remote_copy(
            src_ref=src,
            dst_ref=dst,
            send_sem=sends,
            recv_sem=receives,
            device_id={"blk": target},
            device_id_type=pl.DeviceIdType.MESH,
        )

    def lend_copies():
        return (
            remote(bias.at[missing], guest_bias, lend_send.at[0], lend_recv.at[0], server),
            remote(q_vmem.at[:, pl.ds(0, lent * DH)], guest_q, lend_send.at[1], lend_recv.at[1], server),
        )

    def back_copy(h):
        return remote(back.at[h], given.at[h], lend_send.at[2], back_recv.at[h], guest)

    def stats_copy():
        return remote(back_stats, given_stats, lend_send.at[3], lend_recv.at[2], guest)

    def when(condition, action):
        if condition is None:
            action()
        else:
            pl.when(condition)(action)

    def start(flows, h):
        for index, src, dst, target, condition in flows:
            when(condition, lambda: flow(index, src, dst, target, h).start())

    def arrive(slot, sender, condition, h):
        when(condition, lambda: received(slot, sender, h).wait_recv())

    barrier = pltpu.get_barrier_semaphore()
    for target, condition in ((d + 4, has_up), (d - 4, has_down), (pair, None), (mate, None)):
        when(
            condition,
            lambda: pl.semaphore_signal(
                barrier, inc=1, device_id={"blk": target}, device_id_type=pl.DeviceIdType.MESH
            ),
        )
    ahead = min(AHEAD, heads)
    for h in range(ahead):
        for c in local_copies(h):
            c.start()
    pl.semaphore_wait(barrier, 2 + has_up.astype(jnp.int32) + has_down.astype(jnp.int32))

    def send_own(h):
        @pl.when(h + ahead < heads)
        def _():
            for c in local_copies(h + ahead):
                c.start()

        for c in local_copies(h):
            c.wait()
        start((own_up, own_down), h)

        @pl.when(jnp.logical_or(crossed, h < held))
        def _():
            start((own_pair,), h)

        start((own_mate,), h)

    first = min(FIRST, heads)
    for h in range(first):
        send_own(jnp.int32(h))

    q_copy = pltpu.make_async_copy(q_hbm, q_vmem, q_sem)
    q_copy.start()
    kept_copy = pltpu.make_async_copy(kept_hbm, kept_ref, kept_sem)
    kept_copy.start()

    def prepare():
        kept_copy.wait()
        for query_slot in range(local_blocks):
            kept = [kept_ref[query_slot, j] for j in range(kept_ref.shape[1])]
            for slot, offset in enumerate(OFFSETS):
                inside = jnp.logical_and(d + offset >= 0, d + offset < n)
                for key_slot in range(local_blocks):
                    block = (d + offset) * local_blocks + key_slot
                    allowed = functools.reduce(jnp.logical_or, [j == block for j in kept])
                    bias[slot, pl.ds(query_slot, 1), pl.ds(key_slot * BLOCK, BLOCK)] = jnp.full(
                        (1, BLOCK), jnp.where(jnp.logical_and(allowed, inside), 0.0, MASKED), jnp.float32
                    )
        q_copy.wait()

    prepare()

    @pl.when(lends)
    def _():
        for c in lend_copies():
            c.start()

    @pl.loop(first, heads)
    def _(h):
        send_own(h)

    for slot, offset in enumerate(OFFSETS[:OWN]):
        source = d + offset

        @pl.when(jnp.logical_or(source < 0, source >= n))
        def _():
            @pl.loop(0, heads)
            def _(h):
                kv[slot, h] = jnp.zeros(kv.shape[2:], kv.dtype)

    @pl.when(lends)
    def _():
        @pl.loop(0, lent)
        def _(h):
            kv[missing, h] = jnp.zeros(kv.shape[2:], kv.dtype)

    @pl.when(serves)
    def _():
        back_stats[...] = jnp.zeros(back_stats.shape, back_stats.dtype)
        for c in lend_copies():
            c.wait_recv()

    def part(q, h, slots, mask):
        tops = [None] * local_blocks
        for i, slot in enumerate(slots):
            s = lax.dot_general(
                q, kv[slot, h, 0], (((1,), (1,)), ((), ())), preferred_element_type=jnp.float32
            )
            for b in range(local_blocks):
                masked = s[b * BLOCK : (b + 1) * BLOCK] + mask(slot, b)
                scores[i, b * BLOCK : (b + 1) * BLOCK] = masked
                tops[b] = masked if tops[b] is None else jnp.maximum(tops[b], masked)
        return jnp.concatenate([jnp.max(t, axis=1, keepdims=True) for t in tops], axis=0)

    def weigh(h, slots, top):
        sums = None
        numerator = None
        for i, slot in enumerate(slots):
            weight = jnp.exp2((scores[i] - top) * C_EXP)
            sums = weight if sums is None else sums + weight
            term = jnp.dot(
                weight.astype(jnp.bfloat16), kv[slot, h, 1], preferred_element_type=jnp.float32
            )
            numerator = term if numerator is None else numerator + term
        return jnp.sum(sums, axis=1, keepdims=True), numerator

    lane = lax.broadcasted_iota(jnp.int32, back_stats.shape, 1)

    def serve(h):
        top = part(guest_q[:, columns(h)], h, (served,), lambda slot, b: guest_bias[b : b + 1, :])
        total, numerator = weigh(h, (served,), top)
        back[h] = numerator.astype(back.dtype)
        stats = jnp.where(lane == h, top, back_stats[...])
        back_stats[...] = jnp.where(lane == h + lent, total, stats)
        back_copy(h).start()

        @pl.when(h == lent - 1)
        def _():
            stats_copy().start()

    def hand_over(h):
        arrive(2 + odd, pair, hand_on[-1], h)
        start((hand_on,), h)

    @pl.loop(0, heads)
    def _(h):
        arrive(5, d - 4, has_down, h)
        arrive(4, d + 4, has_up, h)
        start(pass_flows[2:], h)

        @pl.when(jnp.logical_or(h >= lent, jnp.logical_not(serves_high)))
        def _():
            start(pass_flows[:1], h)

        @pl.when(jnp.logical_or(h >= lent, jnp.logical_not(serves_low)))
        def _():
            start(pass_flows[1:2], h)

        @pl.when(jnp.logical_and(serves, h < lent))
        def _():
            serve(h)

        @pl.when(straight)
        def _():
            hand_over(h)

        @pl.when(jnp.logical_and(crossed, h >= lag))
        def _():
            hand_over(h - lag)

    @pl.when(straight)
    def _():
        @pl.loop(held, heads)
        def _(h):
            start((own_pair,), h)

    early = (OWN, 4, 5, 0, 1, 2 + odd)
    late = (3 - odd, 6, 7)

    @pl.loop(0, heads)
    def _(h):
        @pl.when(jnp.logical_and(crossed, h + heads - lag < heads))
        def _():
            hand_over(h + heads - lag)

        borrowed = jnp.logical_and(lends, h < lent)
        lacking = jnp.where(borrowed, missing, -1)

        def mask(slot, b):
            return bias[slot, b : b + 1, :] + jnp.where(slot == lacking, MASKED, 0.0)

        q = q_vmem[:, columns(h)]
        arrive(odd, mate, None, h)
        arrive(1 - odd, mate, jnp.where(odd == 1, d + 1 < n, d - 1 >= 0), h)
        top_early = part(q, h, early, lambda slot, b: bias[slot, b : b + 1, :])
        total_early, numerator_early = weigh(h, early, top_early)

        arrive(3 - odd, pair, jnp.where(odd == 1, d + 2 < n, d - 2 >= 0), h)
        arrive(7, d - 4, jnp.logical_and(d - 8 >= 0, lacking != 7), h)
        arrive(6, d + 4, jnp.logical_and(d + 8 < n, lacking != 6), h)
        top = jnp.maximum(top_early, part(q, h, late, mask))
        total, numerator = weigh(h, late, top)
        shrink = jnp.exp2((top_early - top) * C_EXP)
        total = total + total_early * shrink
        numerator = numerator + numerator_early * shrink

        @pl.when(jnp.logical_not(borrowed))
        def _():
            out_ref[:, columns(h)] = (numerator / total).astype(out_ref.dtype)

        @pl.when(borrowed)
        def _():
            @pl.when(h == 0)
            def _():
                stats_copy().wait_recv()

            back_copy(h).wait_recv()
            stats = given_stats[...]
            top_given = jnp.sum(jnp.where(lane == h, stats, 0.0), axis=1, keepdims=True)
            total_given = jnp.sum(jnp.where(lane == h + lent, stats, 0.0), axis=1, keepdims=True)
            top_all = jnp.maximum(top, top_given)
            here = jnp.exp2((top - top_all) * C_EXP)
            there = jnp.exp2((top_given - top_all) * C_EXP)
            joined = numerator * here + given[h].astype(jnp.float32) * there
            out_ref[:, columns(h)] = (joined / (total * here + total_given * there)).astype(out_ref.dtype)

    for index, src, dst, target, condition in (own_up, own_down, own_pair, own_mate, pass_flows[2], hand_on):
        when(condition, lambda: sent(index, src, target, 0).wait_send())
    for (index, src, dst, target, condition), short in (
        (pass_flows[0], serves_high), (pass_flows[1], serves_low)
    ):
        for skipped, met in ((0, jnp.logical_not(short)), (lent, short)):
            when(
                jnp.logical_and(condition, met),
                lambda: sent(index, src, target, skipped).wait_send(),
            )

    @pl.when(lends)
    def _():
        for c in lend_copies():
            c.wait_send()

    @pl.when(serves)
    def _():
        remote(back, given, lend_send.at[2], back_recv.at[0], guest).wait_send()
        stats_copy().wait_send()


def per_device(queries, keys, values, kept_blocks):
    n = lax.axis_size("blk")
    rows, features = queries.shape
    heads = features // DH
    slots = len(OFFSETS)
    lent = min(LENT, heads)
    inputs = [
        pltpu.with_memory_space_constraint(x, pltpu.HBM) for x in (kept_blocks, queries, keys, values)
    ]
    return pl.pallas_call(
        functools.partial(kernel, n, heads, lent),
        out_shape=jax.ShapeDtypeStruct((rows, features), jnp.bfloat16),
        in_specs=[pl.BlockSpec(memory_space=pltpu.HBM)] * 4,
        out_specs=pl.BlockSpec(memory_space=pltpu.VMEM),
        scratch_shapes=[
            pltpu.VMEM((slots, heads, 2, rows, DH), jnp.bfloat16),
            pltpu.SMEM(kept_blocks.shape, jnp.int32),
            pltpu.VMEM((rows, features), jnp.bfloat16),
            pltpu.VMEM((6, rows, rows), jnp.float32),
            pltpu.VMEM((slots, rows // BLOCK, rows), jnp.float32),
            pltpu.VMEM((rows, lent * DH), jnp.bfloat16),
            pltpu.VMEM((rows // BLOCK, rows), jnp.float32),
            pltpu.VMEM((lent, rows, DH), jnp.bfloat16),
            pltpu.VMEM((rows, DH), jnp.float32),
            pltpu.VMEM((lent, rows, DH), jnp.bfloat16),
            pltpu.VMEM((rows, DH), jnp.float32),
            pltpu.SemaphoreType.DMA((2, heads)),
            pltpu.SemaphoreType.DMA,
            pltpu.SemaphoreType.DMA,
            pltpu.SemaphoreType.DMA((8,)),
            pltpu.SemaphoreType.DMA((8, heads)),
            pltpu.SemaphoreType.DMA((4,)),
            pltpu.SemaphoreType.DMA((3,)),
            pltpu.SemaphoreType.DMA((lent,)),
        ],
        compiler_params=pltpu.CompilerParams(
            collective_id=0, has_side_effects=True, vmem_limit_bytes=40 * 2**20
        ),
    )(*inputs)


def solution(mesh):
    placed = P(("clip", "blk"), None)
    return jax.shard_map(
        per_device, mesh=mesh, in_specs=(placed,) * 4, out_specs=placed, check_vma=False
    )
```

```python
import functools
import math

import jax
import jax.numpy as jnp
from jax import lax
from jax.experimental import pallas as pl
from jax.experimental.pallas import tpu as pltpu
from jax.sharding import PartitionSpec as P

DH = 128
BLOCK = 128
GROUP = 4
TAIL = (2, 2, 1, 1, 1, 1)
LENT = 4
HELD = 8

OFFSETS = (1, -1, 2, -2, 4, -4, 8, -8, 0)
OWN = 8
MASKED = -1e30
C_EXP = math.log2(math.e) / math.sqrt(DH)


def spans(heads, tail):
    sizes = [GROUP] * ((heads - sum(tail)) // GROUP) + list(tail)
    return [(sum(sizes[:i]), size) for i, size in enumerate(sizes)]


def kernel(
    n, heads, lent, kept_hbm, q_hbm, k_hbm, v_hbm, out_ref,
    kv, kept_ref, q_vmem, scores, bias, guest_q, guest_bias, back, back_stats, given, given_stats,
    local_sem, kept_sem, q_sem, send_sem, coarse_recv, fine_recv, far_recv, lend_send, lend_recv,
):
    rows = kv.shape[-2]
    local_blocks = rows // BLOCK
    d = lax.axis_index("blk")
    r = lax.rem(d, 4)
    upper = r // 2
    odd = lax.rem(r, 2)
    straight = odd == upper
    crossed = odd != upper

    pair = d + 2 - 4 * upper
    mate = d + 1 - 2 * odd
    has_up = d + 4 < n
    has_down = d - 4 >= 0
    both = jnp.logical_and(has_up, has_down)

    low, high = d < 4, d + 4 >= n
    serves_low = jnp.logical_and(d >= 4, d < 8)
    serves_high = jnp.logical_and(d + 4 < n, d + 8 >= n)
    lends = jnp.logical_or(low, high)
    serves = jnp.logical_or(serves_low, serves_high)
    server = jnp.where(low, d + 4, d - 4)
    guest = jnp.where(serves_low, d - 4, d + 4)
    missing = jnp.where(low, 6, 7)
    served = jnp.where(serves_low, 4, 5)

    coarse = spans(heads, ())
    fine = spans(heads, TAIL)
    lag = HELD // GROUP

    def columns(h):
        return pl.ds(pl.multiple_of(h * DH, DH), DH)

    def load(j):
        first, size = coarse[j]

        @pl.loop(first, first + size)
        def _(h):
            for i, hbm in ((0, k_hbm), (1, v_hbm)):
                pltpu.make_async_copy(hbm.at[:, columns(h)], kv.at[OWN, h, i], local_sem.at[j]).start()

    def loaded(j):
        group = kv.at[OWN, pl.ds(*coarse[j])]
        pltpu.make_async_copy(group, group, local_sem.at[j]).wait()

    def sem_of(slot, g, is_fine):
        if is_fine == "far":
            return far_recv.at[g]
        return fine_recv.at[slot - 2, g] if is_fine else coarse_recv.at[jnp.where(slot < 2, slot, slot - 2), g]

    def flow(index, src_slot, dst_slot, target, span, g, is_fine):
        return pltpu.make_async_remote_copy(
            src_ref=kv.at[src_slot, pl.ds(*span)],
            dst_ref=kv.at[dst_slot, pl.ds(*span)],
            send_sem=send_sem.at[index],
            recv_sem=sem_of(dst_slot, g, is_fine),
            device_id={"blk": target},
            device_id_type=pl.DeviceIdType.MESH,
        )

    def received(group, sem, sender):
        return pltpu.make_async_remote_copy(
            src_ref=group,
            dst_ref=group,
            send_sem=send_sem.at[0],
            recv_sem=sem,
            device_id={"blk": sender},
            device_id_type=pl.DeviceIdType.MESH,
        )

    def sent(index, src_slot, target, skipped):
        some = pl.ds(skipped, heads - skipped)
        return pltpu.make_async_remote_copy(
            src_ref=kv.at[src_slot, some],
            dst_ref=kv.at[src_slot, some],
            send_sem=send_sem.at[index],
            recv_sem=coarse_recv.at[0, 0],
            device_id={"blk": target},
            device_id_type=pl.DeviceIdType.MESH,
        )

    own_up = (0, OWN, 5, d + 4, has_up)
    own_down = (1, OWN, 4, d - 4, has_down)
    own_pair = (2, OWN, 3 - upper, pair, None)
    own_mate = (3, OWN, 1 - odd, mate, None)
    pass_up = (4, 5, 7, d + 4, both)
    pass_down = (5, 4, 6, d - 4, both)
    pass_pair = (6, 4 + upper, 2 + upper, pair, jnp.where(upper == 1, d - 4 >= 0, d + 4 < n))
    hand_on = (7, 2 + odd, odd, mate, jnp.where(odd == 1, d - 2 >= 0, d + 2 < n))

    def remote(src, dst, sends, receives, target):
        return pltpu.make_async_remote_copy(
            src_ref=src,
            dst_ref=dst,
            send_sem=sends,
            recv_sem=receives,
            device_id={"blk": target},
            device_id_type=pl.DeviceIdType.MESH,
        )

    def lend_copies():
        return (
            remote(bias.at[missing], guest_bias, lend_send.at[0], lend_recv.at[0], server),
            remote(q_vmem.at[:, pl.ds(0, lent * DH)], guest_q, lend_send.at[1], lend_recv.at[1], server),
        )

    def back_copy(span):
        return remote(back.at[pl.ds(*span)], given.at[pl.ds(*span)], lend_send.at[2], lend_recv.at[3], guest)

    def stats_copy():
        return remote(back_stats, given_stats, lend_send.at[3], lend_recv.at[2], guest)

    def when(condition, action):
        if condition is None:
            action()
        else:
            pl.when(condition)(action)

    def start(a_flow, g, is_fine):
        *rest, condition = a_flow
        span = fine[g] if is_fine else coarse[g]
        when(condition, lambda: flow(*rest, span, g, is_fine).start())

    def arrive(slot, sender, condition, g, is_fine):
        group = kv.at[slot, pl.ds(*(fine[g] if is_fine else coarse[g]))]
        when(condition, lambda: received(group, sem_of(slot, g, is_fine), sender).wait_recv())

    def within(j):
        first, size = coarse[j]
        return [g for g, (start, _) in enumerate(fine) if first <= start < first + size]

    barrier = pltpu.get_barrier_semaphore()
    for target, condition in ((d + 4, has_up), (d - 4, has_down), (pair, None), (mate, None)):
        when(
            condition,
            lambda: pl.semaphore_signal(
                barrier, inc=1, device_id={"blk": target}, device_id_type=pl.DeviceIdType.MESH
            ),
        )
    load(0)
    pl.semaphore_wait(barrier, 2 + has_up.astype(jnp.int32) + has_down.astype(jnp.int32))

    def send_own(j):
        if j + 1 < len(coarse):
            load(j + 1)
        loaded(j)
        start(own_up, j, False)
        start(own_down, j, False)
        if coarse[j][0] < HELD:
            for g in within(j):
                start(own_pair, g, True)
        else:

            @pl.when(crossed)
            def _():
                for g in within(j):
                    start(own_pair, g, True)

        start(own_mate, j, False)

    send_own(0)

    q_copy = pltpu.make_async_copy(q_hbm, q_vmem, q_sem)
    q_copy.start()
    kept_copy = pltpu.make_async_copy(kept_hbm, kept_ref, kept_sem)
    kept_copy.start()

    def prepare():
        kept_copy.wait()
        for query_slot in range(local_blocks):
            kept = [kept_ref[query_slot, j] for j in range(kept_ref.shape[1])]
            for slot, offset in enumerate(OFFSETS):
                inside = jnp.logical_and(d + offset >= 0, d + offset < n)
                for key_slot in range(local_blocks):
                    block = (d + offset) * local_blocks + key_slot
                    allowed = functools.reduce(jnp.logical_or, [j == block for j in kept])
                    bias[slot, pl.ds(query_slot, 1), pl.ds(key_slot * BLOCK, BLOCK)] = jnp.full(
                        (1, BLOCK), jnp.where(jnp.logical_and(allowed, inside), 0.0, MASKED), jnp.float32
                    )
        q_copy.wait()

    prepare()

    @pl.when(lends)
    def _():
        for c in lend_copies():
            c.start()

    for j in range(1, len(coarse)):
        send_own(j)

    for slot, offset in enumerate(OFFSETS[:OWN]):
        source = d + offset

        @pl.when(jnp.logical_or(source < 0, source >= n))
        def _():
            @pl.loop(0, heads)
            def _(h):
                kv[slot, h] = jnp.zeros(kv.shape[2:], kv.dtype)

    @pl.when(lends)
    def _():
        @pl.loop(0, lent)
        def _(h):
            kv[missing, h] = jnp.zeros(kv.shape[2:], kv.dtype)

    @pl.when(serves)
    def _():
        back_stats[...] = jnp.zeros(back_stats.shape, back_stats.dtype)
        for c in lend_copies():
            c.wait_recv()

    def part(q, h, slots, mask):
        tops = [None] * local_blocks
        for i, slot in enumerate(slots):
            s = lax.dot_general(
                q, kv[slot, h, 0], (((1,), (1,)), ((), ())), preferred_element_type=jnp.float32
            )
            for b in range(local_blocks):
                masked = s[b * BLOCK : (b + 1) * BLOCK] + mask(slot, b)
                scores[i, b * BLOCK : (b + 1) * BLOCK] = masked
                tops[b] = masked if tops[b] is None else jnp.maximum(tops[b], masked)
        return jnp.concatenate([jnp.max(t, axis=1, keepdims=True) for t in tops], axis=0)

    def weigh(h, slots, top):
        sums = None
        numerator = None
        for i, slot in enumerate(slots):
            weight = jnp.exp2((scores[i] - top) * C_EXP)
            sums = weight if sums is None else sums + weight
            term = jnp.dot(
                weight.astype(jnp.bfloat16), kv[slot, h, 1], preferred_element_type=jnp.float32
            )
            numerator = term if numerator is None else numerator + term
        return jnp.sum(sums, axis=1, keepdims=True), numerator

    lane = lax.broadcasted_iota(jnp.int32, back_stats.shape, 1)

    def serve(h):
        top = part(guest_q[:, columns(h)], h, (served,), lambda slot, b: guest_bias[b : b + 1, :])
        total, numerator = weigh(h, (served,), top)
        back[h] = numerator.astype(back.dtype)
        stats = jnp.where(lane == h, top, back_stats[...])
        back_stats[...] = jnp.where(lane == h + lent, total, stats)

    def hand_over(j):
        for g in within(j):
            arrive(2 + odd, pair, hand_on[-1], g, True)
        start(hand_on, j, False)

    for j, span in enumerate(coarse):
        arrive(5, d - 4, has_down, j, False)
        arrive(4, d + 4, has_up, j, False)
        for g in within(j):
            start(pass_pair, g, True)
        if span[0] < lent:
            for a_flow, serving in ((pass_up, serves_high), (pass_down, serves_low)):

                @pl.when(jnp.logical_not(serving))
                def _():
                    for g in within(j):
                        start(a_flow, g, "far")

            @pl.when(serves)
            def _():
                pl.loop(span[0], sum(span))(serve)
                back_copy(span).start()
                if sum(span) == lent:
                    stats_copy().start()
        else:
            for g in within(j):
                start(pass_up, g, "far")
                start(pass_down, g, "far")

        @pl.when(straight)
        def _():
            hand_over(j)

        if j >= lag:

            @pl.when(crossed)
            def _():
                hand_over(j - lag)

    @pl.when(straight)
    def _():
        for g, (first, _) in enumerate(fine):
            if first >= HELD:
                start(own_pair, g, True)

    early = (OWN, 4, 5, 0, 1, 2 + odd)
    far = (6, 7) if n > 16 else (jnp.where(d - 8 >= 0, 7, 6),)
    late = (3 - odd, *far)

    @pl.loop(0, heads)
    def _(h):
        for j, (first, _) in enumerate(coarse):

            @pl.when(h == first)
            def _():
                if 1 <= j <= lag:

                    @pl.when(crossed)
                    def _():
                        hand_over(len(coarse) - lag - 1 + j)

                arrive(odd, mate, None, j, False)
                arrive(1 - odd, mate, jnp.where(odd == 1, d + 1 < n, d - 1 >= 0), j, False)

        borrowed = jnp.logical_and(lends, h < lent)
        lacking = jnp.where(borrowed, missing, -1)

        def mask(slot, b):
            return bias[slot, b : b + 1, :] + jnp.where(slot == lacking, MASKED, 0.0)

        q = q_vmem[:, columns(h)]
        top_early = part(q, h, early, lambda slot, b: bias[slot, b : b + 1, :])
        total_early, numerator_early = weigh(h, early, top_early)

        for g, (first, size) in enumerate(fine):

            @pl.when(h == first)
            def _():
                arrive(3 - odd, pair, jnp.where(odd == 1, d + 2 < n, d - 2 >= 0), g, True)
                down, up = d - 8 >= 0, d + 8 < n
                if first < lent:
                    down = jnp.logical_and(down, jnp.logical_not(high))
                    up = jnp.logical_and(up, jnp.logical_not(low))
                two = jnp.logical_and(down, up)
                one = jnp.logical_xor(down, up)
                single = kv.at[6, pl.ds(first, size)]
                when(one, lambda: received(single, far_recv.at[g], mate).wait_recv())
                if n > 16:
                    double = kv.at[pl.ds(6, 2), pl.ds(first, size)]
                    when(two, lambda: received(double, far_recv.at[g], mate).wait_recv())

        top = jnp.maximum(top_early, part(q, h, late, mask))
        total, numerator = weigh(h, late, top)
        shrink = jnp.exp2((top_early - top) * C_EXP)
        total = total + total_early * shrink
        numerator = numerator + numerator_early * shrink

        @pl.when(jnp.logical_not(borrowed))
        def _():
            out_ref[:, columns(h)] = (numerator / total).astype(out_ref.dtype)

        @pl.when(borrowed)
        def _():
            @pl.when(h == 0)
            def _():
                back_copy((0, lent)).wait_recv()
                stats_copy().wait_recv()

            stats = given_stats[...]
            top_given = jnp.sum(jnp.where(lane == h, stats, 0.0), axis=1, keepdims=True)
            total_given = jnp.sum(jnp.where(lane == h + lent, stats, 0.0), axis=1, keepdims=True)
            top_all = jnp.maximum(top, top_given)
            here = jnp.exp2((top - top_all) * C_EXP)
            there = jnp.exp2((top_given - top_all) * C_EXP)
            joined = numerator * here + given[h].astype(jnp.float32) * there
            out_ref[:, columns(h)] = (joined / (total * here + total_given * there)).astype(out_ref.dtype)

    for index, src, dst, target, condition in (own_up, own_down, own_pair, own_mate, pass_pair, hand_on):
        when(condition, lambda: sent(index, src, target, 0).wait_send())
    for (index, src, dst, target, condition), short in (
        (pass_up, serves_high), (pass_down, serves_low)
    ):
        for skipped, met in ((0, jnp.logical_not(short)), (lent, short)):
            when(
                jnp.logical_and(condition, met),
                lambda: sent(index, src, target, skipped).wait_send(),
            )

    @pl.when(lends)
    def _():
        for c in lend_copies():
            c.wait_send()

    @pl.when(serves)
    def _():
        back_copy((0, lent)).wait_send()
        stats_copy().wait_send()


def per_device(queries, keys, values, kept_blocks):
    n = lax.axis_size("blk")
    rows, features = queries.shape
    heads = features // DH
    slots = len(OFFSETS)
    lent = min(LENT, heads)
    coarse, fine = len(spans(heads, ())), len(spans(heads, TAIL))
    inputs = [
        pltpu.with_memory_space_constraint(x, pltpu.HBM) for x in (kept_blocks, queries, keys, values)
    ]
    return pl.pallas_call(
        functools.partial(kernel, n, heads, lent),
        out_shape=jax.ShapeDtypeStruct((rows, features), jnp.bfloat16),
        in_specs=[pl.BlockSpec(memory_space=pltpu.HBM)] * 4,
        out_specs=pl.BlockSpec(memory_space=pltpu.VMEM),
        scratch_shapes=[
            pltpu.VMEM((slots, heads, 2, rows, DH), jnp.bfloat16),
            pltpu.SMEM(kept_blocks.shape, jnp.int32),
            pltpu.VMEM((rows, features), jnp.bfloat16),
            pltpu.VMEM((6, rows, rows), jnp.float32),
            pltpu.VMEM((slots, rows // BLOCK, rows), jnp.float32),
            pltpu.VMEM((rows, lent * DH), jnp.bfloat16),
            pltpu.VMEM((rows // BLOCK, rows), jnp.float32),
            pltpu.VMEM((lent, rows, DH), jnp.bfloat16),
            pltpu.VMEM((rows, DH), jnp.float32),
            pltpu.VMEM((lent, rows, DH), jnp.bfloat16),
            pltpu.VMEM((rows, DH), jnp.float32),
            pltpu.SemaphoreType.DMA((coarse,)),
            pltpu.SemaphoreType.DMA,
            pltpu.SemaphoreType.DMA,
            pltpu.SemaphoreType.DMA((8,)),
            pltpu.SemaphoreType.DMA((4, coarse)),
            pltpu.SemaphoreType.DMA((2, fine)),
            pltpu.SemaphoreType.DMA((fine,)),
            pltpu.SemaphoreType.DMA((4,)),
            pltpu.SemaphoreType.DMA((4,)),
        ],
        compiler_params=pltpu.CompilerParams(
            collective_id=0, has_side_effects=True, vmem_limit_bytes=40 * 2**20
        ),
    )(*inputs)


def solution(mesh):
    placed = P(("clip", "blk"), None)
    return jax.shard_map(
        per_device, mesh=mesh, in_specs=(placed,) * 4, out_specs=placed, check_vma=False
    )
```

```python
import functools
import math

import jax
import jax.numpy as jnp
from jax import lax
from jax.experimental import pallas as pl
from jax.experimental.pallas import tpu as pltpu
from jax.sharding import PartitionSpec as P

DH = 128
BLOCK = 128
GROUP = 4
TAIL = (2, 2, 1, 1, 1, 1)
LENT = 4
HELD = 8

OFFSETS = (1, -1, 2, -2, 4, -4, 8, -8, 0)
OWN = 8
MASKED = -1e30
C_EXP = math.log2(math.e) / math.sqrt(DH)


def spans(heads, tail):
    sizes = [GROUP] * ((heads - sum(tail)) // GROUP) + list(tail)
    return [(sum(sizes[:i]), size) for i, size in enumerate(sizes)]


def kernel(
    n, heads, lent, kept_hbm, q_hbm, k_hbm, v_hbm, out_ref,
    kv, kept_ref, q_vmem, scores, bias, guest_q, guest_bias, back, back_stats, given, given_stats,
    local_sem, kept_sem, q_sem, send_sem, coarse_recv, fine_recv, far_recv, lend_send, lend_recv,
):
    rows = kv.shape[-2]
    local_blocks = rows // BLOCK
    d = lax.axis_index("blk")
    r = lax.rem(d, 4)
    upper = r // 2
    odd = lax.rem(r, 2)
    straight = odd == upper
    crossed = odd != upper

    pair = d + 2 - 4 * upper
    mate = d + 1 - 2 * odd
    has_up = d + 4 < n
    has_down = d - 4 >= 0
    both = jnp.logical_and(has_up, has_down)

    low, high = d < 4, d + 4 >= n
    serves_low = jnp.logical_and(d >= 4, d < 8)
    serves_high = jnp.logical_and(d + 4 < n, d + 8 >= n)
    lends = jnp.logical_or(low, high)
    serves = jnp.logical_or(serves_low, serves_high)
    server = jnp.where(low, d + 4, d - 4)
    guest = jnp.where(serves_low, d - 4, d + 4)
    missing = jnp.where(low, 6, 7)
    served = jnp.where(serves_low, 4, 5)

    coarse = spans(heads, ())
    fine = spans(heads, TAIL)
    lag = HELD // GROUP

    def columns(h):
        return pl.ds(pl.multiple_of(h * DH, DH), DH)

    def load(j):
        first, size = coarse[j]

        @pl.loop(first, first + size)
        def _(h):
            for i, hbm in ((0, k_hbm), (1, v_hbm)):
                pltpu.make_async_copy(hbm.at[:, columns(h)], kv.at[OWN, h, i], local_sem.at[j]).start()

    def loaded(j):
        group = kv.at[OWN, pl.ds(*coarse[j])]
        pltpu.make_async_copy(group, group, local_sem.at[j]).wait()

    def sem_of(slot, g, is_fine):
        if is_fine == "far":
            return far_recv.at[g]
        return fine_recv.at[slot - 2, g] if is_fine else coarse_recv.at[jnp.where(slot < 2, slot, slot - 2), g]

    last = len(fine) - 1

    def heads_of(slot, g, is_fine):
        if is_fine and g >= last:
            return kv.at[slot, fine[last][0], g - last]
        return kv.at[slot, pl.ds(*(fine[g] if is_fine else coarse[g]))]

    def flow(index, src_slot, dst_slot, target, g, is_fine):
        return pltpu.make_async_remote_copy(
            src_ref=heads_of(src_slot, g, is_fine),
            dst_ref=heads_of(dst_slot, g, is_fine),
            send_sem=send_sem.at[index],
            recv_sem=sem_of(dst_slot, g, is_fine),
            device_id={"blk": target},
            device_id_type=pl.DeviceIdType.MESH,
        )

    def received(group, sem, sender):
        return pltpu.make_async_remote_copy(
            src_ref=group,
            dst_ref=group,
            send_sem=send_sem.at[0],
            recv_sem=sem,
            device_id={"blk": sender},
            device_id_type=pl.DeviceIdType.MESH,
        )

    def sent(index, src_slot, target, skipped):
        some = pl.ds(skipped, heads - skipped)
        return pltpu.make_async_remote_copy(
            src_ref=kv.at[src_slot, some],
            dst_ref=kv.at[src_slot, some],
            send_sem=send_sem.at[index],
            recv_sem=coarse_recv.at[0, 0],
            device_id={"blk": target},
            device_id_type=pl.DeviceIdType.MESH,
        )

    own_up = (0, OWN, 5, d + 4, has_up)
    own_down = (1, OWN, 4, d - 4, has_down)
    own_pair = (2, OWN, 3 - upper, pair, None)
    own_mate = (3, OWN, 1 - odd, mate, None)
    pass_up = (4, 5, 7, d + 4, both)
    pass_down = (5, 4, 6, d - 4, both)
    pass_pair = (6, 4 + upper, 2 + upper, pair, jnp.where(upper == 1, d - 4 >= 0, d + 4 < n))
    hand_on = (7, 2 + odd, odd, mate, jnp.where(odd == 1, d - 2 >= 0, d + 2 < n))

    def remote(src, dst, sends, receives, target):
        return pltpu.make_async_remote_copy(
            src_ref=src,
            dst_ref=dst,
            send_sem=sends,
            recv_sem=receives,
            device_id={"blk": target},
            device_id_type=pl.DeviceIdType.MESH,
        )

    def lend_copies():
        return (
            remote(bias.at[missing], guest_bias, lend_send.at[0], lend_recv.at[0], server),
            remote(q_vmem.at[:, pl.ds(0, lent * DH)], guest_q, lend_send.at[1], lend_recv.at[1], server),
        )

    def back_copy(span):
        return remote(back.at[pl.ds(*span)], given.at[pl.ds(*span)], lend_send.at[2], lend_recv.at[3], guest)

    def stats_copy():
        return remote(back_stats, given_stats, lend_send.at[3], lend_recv.at[2], guest)

    def when(condition, action):
        if condition is None:
            action()
        else:
            pl.when(condition)(action)

    def start(a_flow, g, is_fine):
        *rest, condition = a_flow
        when(condition, lambda: flow(*rest, g, is_fine).start())

    def arrive(slot, sender, condition, g, is_fine):
        group = heads_of(slot, g, is_fine)
        when(condition, lambda: received(group, sem_of(slot, g, is_fine), sender).wait_recv())

    def within(j):
        first, size = coarse[j]
        groups = [g for g, (start, _) in enumerate(fine) if first <= start < first + size]
        return groups + [last + 1] * (last in groups)

    barrier = pltpu.get_barrier_semaphore()
    for target, condition in ((d + 4, has_up), (d - 4, has_down), (pair, None), (mate, None)):
        when(
            condition,
            lambda: pl.semaphore_signal(
                barrier, inc=1, device_id={"blk": target}, device_id_type=pl.DeviceIdType.MESH
            ),
        )
    for j in range(min(2, len(coarse))):
        load(j)
    pl.semaphore_wait(barrier, 2 + has_up.astype(jnp.int32) + has_down.astype(jnp.int32))

    def send_own(j):
        loaded(j)
        start(own_up, j, False)
        start(own_down, j, False)
        if coarse[j][0] < HELD:
            for g in within(j):
                start(own_pair, g, True)
        else:

            @pl.when(crossed)
            def _():
                for g in within(j):
                    start(own_pair, g, True)

        start(own_mate, j, False)
        if j + 2 < len(coarse):
            load(j + 2)

    send_own(0)

    q_copy = pltpu.make_async_copy(q_hbm, q_vmem, q_sem)
    q_copy.start()
    kept_copy = pltpu.make_async_copy(kept_hbm, kept_ref, kept_sem)
    kept_copy.start()

    def prepare():
        kept_copy.wait()
        for query_slot in range(local_blocks):
            kept = [kept_ref[query_slot, j] for j in range(kept_ref.shape[1])]
            for slot, offset in enumerate(OFFSETS):
                inside = jnp.logical_and(d + offset >= 0, d + offset < n)
                for key_slot in range(local_blocks):
                    block = (d + offset) * local_blocks + key_slot
                    allowed = functools.reduce(jnp.logical_or, [j == block for j in kept])
                    bias[slot, pl.ds(query_slot, 1), pl.ds(key_slot * BLOCK, BLOCK)] = jnp.full(
                        (1, BLOCK), jnp.where(jnp.logical_and(allowed, inside), 0.0, MASKED), jnp.float32
                    )
        q_copy.wait()

    prepare()

    @pl.when(lends)
    def _():
        for c in lend_copies():
            c.start()

    for j in range(1, len(coarse)):
        send_own(j)

    for slot, offset in enumerate(OFFSETS[:OWN]):
        source = d + offset

        @pl.when(jnp.logical_or(source < 0, source >= n))
        def _():
            @pl.loop(0, heads)
            def _(h):
                kv[slot, h] = jnp.zeros(kv.shape[2:], kv.dtype)

    @pl.when(lends)
    def _():
        @pl.loop(0, lent)
        def _(h):
            kv[missing, h] = jnp.zeros(kv.shape[2:], kv.dtype)

    @pl.when(serves)
    def _():
        back_stats[...] = jnp.zeros(back_stats.shape, back_stats.dtype)
        for c in lend_copies():
            c.wait_recv()

    def part(q, h, slots, mask):
        tops = [None] * local_blocks
        for i, slot in enumerate(slots):
            s = lax.dot_general(
                q, kv[slot, h, 0], (((1,), (1,)), ((), ())), preferred_element_type=jnp.float32
            )
            for b in range(local_blocks):
                masked = s[b * BLOCK : (b + 1) * BLOCK] + mask(slot, b)
                scores[i, b * BLOCK : (b + 1) * BLOCK] = masked
                tops[b] = masked if tops[b] is None else jnp.maximum(tops[b], masked)
        return jnp.concatenate([jnp.max(t, axis=1, keepdims=True) for t in tops], axis=0)

    def weigh(h, slots, top, values_here=None):
        sums = None
        numerator = None
        kept = []
        for i, slot in enumerate(slots):
            weight = jnp.exp2((scores[i] - top) * C_EXP)
            sums = weight if sums is None else sums + weight
            kept.append(weight.astype(jnp.bfloat16))
            if values_here is None:
                term = jnp.dot(kept[i], kv[slot, h, 1], preferred_element_type=jnp.float32)
                numerator = term if numerator is None else numerator + term
        total = jnp.sum(sums, axis=1, keepdims=True)
        if values_here is not None:
            values_here()
            for i, slot in enumerate(slots):
                term = jnp.dot(kept[i], kv[slot, h, 1], preferred_element_type=jnp.float32)
                numerator = term if numerator is None else numerator + term
        return total, numerator

    lane = lax.broadcasted_iota(jnp.int32, back_stats.shape, 1)

    def serve(h):
        top = part(guest_q[:, columns(h)], h, (served,), lambda slot, b: guest_bias[b : b + 1, :])
        total, numerator = weigh(h, (served,), top)
        back[h] = numerator.astype(back.dtype)
        stats = jnp.where(lane == h, top, back_stats[...])
        back_stats[...] = jnp.where(lane == h + lent, total, stats)

    def hand_over(j):
        for g in within(j):
            arrive(2 + odd, pair, hand_on[-1], g, True)
        start(hand_on, j, False)

    for j, span in enumerate(coarse):
        arrive(5, d - 4, has_down, j, False)
        arrive(4, d + 4, has_up, j, False)
        for g in within(j):
            start(pass_pair, g, True)
        if span[0] < lent:
            for a_flow, serving in ((pass_up, serves_high), (pass_down, serves_low)):

                @pl.when(jnp.logical_not(serving))
                def _():
                    for g in within(j):
                        start(a_flow, g, "far")

            @pl.when(serves)
            def _():
                pl.loop(span[0], sum(span))(serve)
                back_copy(span).start()
                if sum(span) == lent:
                    stats_copy().start()
        else:
            for g in within(j):
                start(pass_up, g, "far")
                start(pass_down, g, "far")

        @pl.when(straight)
        def _():
            hand_over(j)

        if j >= lag:

            @pl.when(crossed)
            def _():
                hand_over(j - lag)

    @pl.when(straight)
    def _():
        for j, (first, _) in enumerate(coarse):
            if first >= HELD:
                for g in within(j):
                    start(own_pair, g, True)

    early = (OWN, 4, 5, 0, 1, 2 + odd)
    far = (6, 7) if n > 16 else (jnp.where(d - 8 >= 0, 7, 6),)
    late = (3 - odd, *far)

    def attend_early(h):
        for j, (first, _) in enumerate(coarse):

            @pl.when(h == first)
            def _():
                if 1 <= j <= lag:

                    @pl.when(crossed)
                    def _():
                        hand_over(len(coarse) - lag - 1 + j)

                arrive(odd, mate, None, j, False)
                arrive(1 - odd, mate, jnp.where(odd == 1, d + 1 < n, d - 1 >= 0), j, False)

        top = part(q_vmem[:, columns(h)], h, early, lambda slot, b: bias[slot, b : b + 1, :])
        return top, *weigh(h, early, top)

    def arrive_late(g):
        first, _ = fine[min(g, last)]
        arrive(3 - odd, pair, jnp.where(odd == 1, d + 2 < n, d - 2 >= 0), g, True)
        down, up = d - 8 >= 0, d + 8 < n
        if first < lent:
            down = jnp.logical_and(down, jnp.logical_not(high))
            up = jnp.logical_and(up, jnp.logical_not(low))
        one = jnp.logical_xor(down, up)
        when(one, lambda: received(heads_of(6, g, True), far_recv.at[g], mate).wait_recv())
        if n > 16:
            both_far = heads_of(pl.ds(6, 2), g, True)
            two = jnp.logical_and(down, up)
            when(two, lambda: received(both_far, far_recv.at[g], mate).wait_recv())

    def attend_late(h, lacking, state, values_here=None):
        top_early, total_early, numerator_early = state

        def mask(slot, b):
            return bias[slot, b : b + 1, :] + jnp.where(slot == lacking, MASKED, 0.0)

        top = jnp.maximum(top_early, part(q_vmem[:, columns(h)], h, late, mask))
        shrink = jnp.exp2((top_early - top) * C_EXP)
        total, numerator = weigh(h, late, top, values_here)
        return top, total + total_early * shrink, numerator + numerator_early * shrink

    def one_head(h, state):
        following = attend_early(h + 1)
        for g, (first, size) in enumerate(fine[:last]):

            @pl.when(h == first)
            def _():
                arrive_late(g)

        borrowed = jnp.logical_and(lends, h < lent)
        top, total, numerator = attend_late(h, jnp.where(borrowed, missing, -1), state)

        @pl.when(jnp.logical_not(borrowed))
        def _():
            out_ref[:, columns(h)] = (numerator / total).astype(out_ref.dtype)

        @pl.when(borrowed)
        def _():
            @pl.when(h == 0)
            def _():
                back_copy((0, lent)).wait_recv()
                stats_copy().wait_recv()

            stats = given_stats[...]
            top_given = jnp.sum(jnp.where(lane == h, stats, 0.0), axis=1, keepdims=True)
            total_given = jnp.sum(jnp.where(lane == h + lent, stats, 0.0), axis=1, keepdims=True)
            top_all = jnp.maximum(top, top_given)
            here = jnp.exp2((top - top_all) * C_EXP)
            there = jnp.exp2((top_given - top_all) * C_EXP)
            joined = numerator * here + given[h].astype(jnp.float32) * there
            out_ref[:, columns(h)] = (joined / (total * here + total_given * there)).astype(out_ref.dtype)

        return following

    state = lax.fori_loop(0, heads - 1, one_head, attend_early(jnp.int32(0)))
    arrive_late(last)
    final = jnp.int32(heads - 1)
    _, total, numerator = attend_late(final, -1, state, lambda: arrive_late(last + 1))
    out_ref[:, columns(final)] = (numerator / total).astype(out_ref.dtype)

    for index, src, dst, target, condition in (own_up, own_down, own_pair, own_mate, pass_pair, hand_on):
        when(condition, lambda: sent(index, src, target, 0).wait_send())
    for (index, src, dst, target, condition), short in (
        (pass_up, serves_high), (pass_down, serves_low)
    ):
        for skipped, met in ((0, jnp.logical_not(short)), (lent, short)):
            when(
                jnp.logical_and(condition, met),
                lambda: sent(index, src, target, skipped).wait_send(),
            )

    @pl.when(lends)
    def _():
        for c in lend_copies():
            c.wait_send()

    @pl.when(serves)
    def _():
        back_copy((0, lent)).wait_send()
        stats_copy().wait_send()


def per_device(queries, keys, values, kept_blocks):
    n = lax.axis_size("blk")
    rows, features = queries.shape
    heads = features // DH
    slots = len(OFFSETS)
    lent = min(LENT, heads)
    coarse, fine = len(spans(heads, ())), len(spans(heads, TAIL)) + 1
    inputs = [
        pltpu.with_memory_space_constraint(x, pltpu.HBM) for x in (kept_blocks, queries, keys, values)
    ]
    return pl.pallas_call(
        functools.partial(kernel, n, heads, lent),
        out_shape=jax.ShapeDtypeStruct((rows, features), jnp.bfloat16),
        in_specs=[pl.BlockSpec(memory_space=pltpu.HBM)] * 4,
        out_specs=pl.BlockSpec(memory_space=pltpu.VMEM),
        scratch_shapes=[
            pltpu.VMEM((slots, heads, 2, rows, DH), jnp.bfloat16),
            pltpu.SMEM(kept_blocks.shape, jnp.int32),
            pltpu.VMEM((rows, features), jnp.bfloat16),
            pltpu.VMEM((6, rows, rows), jnp.float32),
            pltpu.VMEM((slots, rows // BLOCK, rows), jnp.float32),
            pltpu.VMEM((rows, lent * DH), jnp.bfloat16),
            pltpu.VMEM((rows // BLOCK, rows), jnp.float32),
            pltpu.VMEM((lent, rows, DH), jnp.bfloat16),
            pltpu.VMEM((rows, DH), jnp.float32),
            pltpu.VMEM((lent, rows, DH), jnp.bfloat16),
            pltpu.VMEM((rows, DH), jnp.float32),
            pltpu.SemaphoreType.DMA((coarse,)),
            pltpu.SemaphoreType.DMA,
            pltpu.SemaphoreType.DMA,
            pltpu.SemaphoreType.DMA((8,)),
            pltpu.SemaphoreType.DMA((4, coarse)),
            pltpu.SemaphoreType.DMA((2, fine)),
            pltpu.SemaphoreType.DMA((fine,)),
            pltpu.SemaphoreType.DMA((4,)),
            pltpu.SemaphoreType.DMA((4,)),
        ],
        compiler_params=pltpu.CompilerParams(
            collective_id=0, has_side_effects=True, vmem_limit_bytes=40 * 2**20
        ),
    )(*inputs)


def solution(mesh):
    placed = P(("clip", "blk"), None)
    return jax.shard_map(
        per_device, mesh=mesh, in_specs=(placed,) * 4, out_specs=placed, check_vma=False
    )
```

```python
import functools
import math

import jax
import jax.numpy as jnp
from jax import lax
from jax.experimental import pallas as pl
from jax.experimental.pallas import tpu as pltpu
from jax.sharding import PartitionSpec as P

DH = 128
BLOCK = 128
GROUP = 4
TAIL = (2, 2, 1, 1, 1, 1)
LENT = 4
HELD = 12

OFFSETS = (1, -1, 2, -2, 4, -4, 8, -8, 0)
OWN = 8
MASKED = -1e30
C_EXP = math.log2(math.e) / math.sqrt(DH)


def spans(heads, tail):
    sizes = [GROUP] * ((heads - sum(tail)) // GROUP) + list(tail)
    return [(sum(sizes[:i]), size) for i, size in enumerate(sizes)]


def kernel(
    n, heads, lent, kept_hbm, q_hbm, k_hbm, v_hbm, out_ref,
    kv, kept_ref, q_vmem, scores, bias, guest_q, guest_bias, back, back_stats, given, given_stats,
    local_sem, kept_sem, q_sem, send_sem, coarse_recv, pair_recv, far_recv, lend_send, lend_recv,
):
    rows = kv.shape[-2]
    local_blocks = rows // BLOCK
    d = lax.axis_index("blk")
    r = lax.rem(d, 4)
    upper = r // 2
    odd = lax.rem(r, 2)
    straight = odd == upper
    crossed = odd != upper

    pair = d + 2 - 4 * upper
    mate = d + 1 - 2 * odd
    has_up = d + 4 < n
    has_down = d - 4 >= 0
    both = jnp.logical_and(has_up, has_down)

    low, high = d < 4, d + 4 >= n
    serves_low = jnp.logical_and(d >= 4, d < 8)
    serves_high = jnp.logical_and(d + 4 < n, d + 8 >= n)
    lends = jnp.logical_or(low, high)
    serves = jnp.logical_or(serves_low, serves_high)
    server = jnp.where(low, d + 4, d - 4)
    guest = jnp.where(serves_low, d - 4, d + 4)
    missing = jnp.where(low, 6, 7)
    served = jnp.where(serves_low, 4, 5)

    coarse = spans(heads, ())
    fine = spans(heads, TAIL)
    lag = HELD // GROUP

    def columns(h):
        return pl.ds(pl.multiple_of(h * DH, DH), DH)

    def load(j):
        first, size = coarse[j]

        @pl.loop(first, first + size)
        def _(h):
            for i, hbm in ((0, k_hbm), (1, v_hbm)):
                pltpu.make_async_copy(hbm.at[:, columns(h)], kv.at[OWN, h, i], local_sem.at[j]).start()

    def loaded(j):
        group = kv.at[OWN, pl.ds(*coarse[j])]
        pltpu.make_async_copy(group, group, local_sem.at[j]).wait()

    def sem_of(kind, g):
        if kind == "far":
            return far_recv.at[g]
        if kind in ("z", "mate"):
            return coarse_recv.at[("z", "mate").index(kind), g]
        first = fine[min(g, last)][0]
        j = max(j for j, span in enumerate(coarse) if span[0] <= first)
        handed = crossed if kind == "own" else straight
        return pair_recv.at[jnp.where(handed, last + 2 + j, g)]

    last = len(fine) - 1

    def heads_of(slot, g, is_fine):
        if is_fine and g >= last:
            return kv.at[slot, fine[last][0], g - last]
        return kv.at[slot, pl.ds(*(fine[g] if is_fine else coarse[g]))]

    def flow(index, src_slot, dst_slot, target, g, kind):
        is_fine = kind not in ("z", "mate")
        return pltpu.make_async_remote_copy(
            src_ref=heads_of(src_slot, g, is_fine),
            dst_ref=heads_of(dst_slot, g, is_fine),
            send_sem=send_sem.at[index],
            recv_sem=sem_of(kind, g),
            device_id={"blk": target},
            device_id_type=pl.DeviceIdType.MESH,
        )

    def received(group, sem, sender):
        return pltpu.make_async_remote_copy(
            src_ref=group,
            dst_ref=group,
            send_sem=send_sem.at[0],
            recv_sem=sem,
            device_id={"blk": sender},
            device_id_type=pl.DeviceIdType.MESH,
        )

    def sent(index, src_slot, target, skipped):
        some = pl.ds(skipped, heads - skipped)
        return pltpu.make_async_remote_copy(
            src_ref=kv.at[src_slot, some],
            dst_ref=kv.at[src_slot, some],
            send_sem=send_sem.at[index],
            recv_sem=coarse_recv.at[0, 0],
            device_id={"blk": target},
            device_id_type=pl.DeviceIdType.MESH,
        )

    own_up = (0, OWN, 5, d + 4, has_up)
    own_down = (1, OWN, 4, d - 4, has_down)
    own_pair = (2, OWN, 3 - upper, pair, None)
    own_mate = (3, OWN, 1 - odd, mate, None)
    pass_up = (4, 5, 7, d + 4, both)
    pass_down = (5, 4, 6, d - 4, both)
    pass_pair = (6, 4 + upper, 2 + upper, pair, jnp.where(upper == 1, d - 4 >= 0, d + 4 < n))
    hand_on = (7, 2 + odd, odd, mate, jnp.where(odd == 1, d - 2 >= 0, d + 2 < n))

    def remote(src, dst, sends, receives, target):
        return pltpu.make_async_remote_copy(
            src_ref=src,
            dst_ref=dst,
            send_sem=sends,
            recv_sem=receives,
            device_id={"blk": target},
            device_id_type=pl.DeviceIdType.MESH,
        )

    def lend_copies():
        return (
            remote(bias.at[missing], guest_bias, lend_send.at[0], lend_recv.at[0], server),
            remote(q_vmem.at[:, pl.ds(0, lent * DH)], guest_q, lend_send.at[1], lend_recv.at[1], server),
        )

    def back_copy(span):
        return remote(back.at[pl.ds(*span)], given.at[pl.ds(*span)], lend_send.at[2], lend_recv.at[3], guest)

    def stats_copy():
        return remote(back_stats, given_stats, lend_send.at[3], lend_recv.at[2], guest)

    def when(condition, action):
        if condition is None:
            action()
        else:
            pl.when(condition)(action)

    def start(a_flow, g, kind):
        *rest, condition = a_flow
        when(condition, lambda: flow(*rest, g, kind).start())

    def within(j):
        first, size = coarse[j]
        groups = [g for g, (start, _) in enumerate(fine) if first <= start < first + size]
        return groups + [last + 1] * (last in groups)

    barrier = pltpu.get_barrier_semaphore()
    for target, condition in ((d + 4, has_up), (d - 4, has_down), (pair, None), (mate, None)):
        when(
            condition,
            lambda: pl.semaphore_signal(
                barrier, inc=1, device_id={"blk": target}, device_id_type=pl.DeviceIdType.MESH
            ),
        )
    for j in range(min(2, len(coarse))):
        load(j)
    pl.semaphore_wait(barrier, 2 + has_up.astype(jnp.int32) + has_down.astype(jnp.int32))

    def send_own(j):
        loaded(j)
        start(own_up, j, "z")
        start(own_down, j, "z")
        if coarse[j][0] < HELD:
            for g in within(j):
                start(own_pair, g, "own")
        else:

            @pl.when(crossed)
            def _():
                for g in within(j):
                    start(own_pair, g, "own")

        start(own_mate, j, "mate")
        if j + 2 < len(coarse):
            load(j + 2)

    send_own(0)

    q_copy = pltpu.make_async_copy(q_hbm, q_vmem, q_sem)
    q_copy.start()
    kept_copy = pltpu.make_async_copy(kept_hbm, kept_ref, kept_sem)
    kept_copy.start()

    def prepare():
        kept_copy.wait()
        for query_slot in range(local_blocks):
            kept = [kept_ref[query_slot, j] for j in range(kept_ref.shape[1])]
            for slot, offset in enumerate(OFFSETS):
                inside = jnp.logical_and(d + offset >= 0, d + offset < n)
                for key_slot in range(local_blocks):
                    block = (d + offset) * local_blocks + key_slot
                    allowed = functools.reduce(jnp.logical_or, [j == block for j in kept])
                    bias[slot, pl.ds(query_slot, 1), pl.ds(key_slot * BLOCK, BLOCK)] = jnp.full(
                        (1, BLOCK), jnp.where(jnp.logical_and(allowed, inside), 0.0, MASKED), jnp.float32
                    )
        q_copy.wait()

    prepare()

    @pl.when(lends)
    def _():
        for c in lend_copies():
            c.start()

    for j in range(1, len(coarse)):
        send_own(j)

    for slot, offset in enumerate(OFFSETS[:OWN]):
        source = d + offset

        @pl.when(jnp.logical_or(source < 0, source >= n))
        def _():
            @pl.loop(0, heads)
            def _(h):
                kv[slot, h] = jnp.zeros(kv.shape[2:], kv.dtype)

    @pl.when(lends)
    def _():
        @pl.loop(0, lent)
        def _(h):
            kv[missing, h] = jnp.zeros(kv.shape[2:], kv.dtype)

    @pl.when(serves)
    def _():
        back_stats[...] = jnp.zeros(back_stats.shape, back_stats.dtype)
        for c in lend_copies():
            c.wait_recv()

    def part(q, h, slots, mask):
        tops = [None] * local_blocks
        for i, slot in enumerate(slots):
            s = lax.dot_general(
                q, kv[slot, h, 0], (((1,), (1,)), ((), ())), preferred_element_type=jnp.float32
            )
            for b in range(local_blocks):
                masked = s[b * BLOCK : (b + 1) * BLOCK] + mask(slot, b)
                scores[i, b * BLOCK : (b + 1) * BLOCK] = masked
                tops[b] = masked if tops[b] is None else jnp.maximum(tops[b], masked)
        return jnp.concatenate([jnp.max(t, axis=1, keepdims=True) for t in tops], axis=0)

    def weigh(h, slots, top, values_here=None):
        sums = None
        numerator = None
        kept = []
        for i, slot in enumerate(slots):
            weight = jnp.exp2((scores[i] - top) * C_EXP)
            sums = weight if sums is None else sums + weight
            kept.append(weight.astype(jnp.bfloat16))
            if values_here is None:
                term = jnp.dot(kept[i], kv[slot, h, 1], preferred_element_type=jnp.float32)
                numerator = term if numerator is None else numerator + term
        total = jnp.sum(sums, axis=1, keepdims=True)
        if values_here is not None:
            values_here()
            for i, slot in enumerate(slots):
                term = jnp.dot(kept[i], kv[slot, h, 1], preferred_element_type=jnp.float32)
                numerator = term if numerator is None else numerator + term
        return total, numerator

    lane = lax.broadcasted_iota(jnp.int32, back_stats.shape, 1)

    def serve(h):
        top = part(guest_q[:, columns(h)], h, (served,), lambda slot, b: guest_bias[b : b + 1, :])
        total, numerator = weigh(h, (served,), top)
        back[h] = numerator.astype(back.dtype)
        stats = jnp.where(lane == h, top, back_stats[...])
        back_stats[...] = jnp.where(lane == h + lent, total, stats)

    def hand_over(j):
        group = kv.at[2 + odd, pl.ds(*coarse[j])]
        when(hand_on[-1], lambda: received(group, pair_recv.at[last + 2 + j], pair).wait_recv())
        start(hand_on, j, "mate")

    for j, span in enumerate(coarse):
        single, double = kv.at[jnp.where(has_up, 4, 5), pl.ds(*span)], kv.at[pl.ds(4, 2), pl.ds(*span)]
        when(both, lambda: received(double, coarse_recv.at[0, j], mate).wait_recv())
        when(jnp.logical_not(both), lambda: received(single, coarse_recv.at[0, j], mate).wait_recv())
        for g in within(j):
            start(pass_pair, g, "pass")
        if span[0] < lent:
            for a_flow, serving in ((pass_up, serves_high), (pass_down, serves_low)):

                @pl.when(jnp.logical_not(serving))
                def _():
                    for g in within(j):
                        start(a_flow, g, "far")

            @pl.when(serves)
            def _():
                pl.loop(span[0], sum(span))(serve)
                back_copy(span).start()
                if sum(span) == lent:
                    stats_copy().start()
        else:
            for g in within(j):
                start(pass_up, g, "far")
                start(pass_down, g, "far")

        @pl.when(straight)
        def _():
            hand_over(j)

        if j >= lag:

            @pl.when(crossed)
            def _():
                hand_over(j - lag)

    @pl.when(straight)
    def _():
        for j, (first, _) in enumerate(coarse):
            if first >= HELD:
                for g in within(j):
                    start(own_pair, g, "own")

    early = (OWN, 4, 5, 0, 1, 2 + odd)
    far = (6, 7) if n > 16 else (jnp.where(d - 8 >= 0, 7, 6),)
    late = (3 - odd, *far)

    def attend_early(h):
        for j, (first, _) in enumerate(coarse):

            @pl.when(h == first)
            def _():
                if 1 <= j <= lag:

                    @pl.when(crossed)
                    def _():
                        hand_over(len(coarse) - lag - 1 + j)

                span = pl.ds(*coarse[j])
                two = jnp.where(odd == 1, d + 1 < n, d - 1 >= 0)
                single, double = kv.at[odd, span], kv.at[pl.ds(0, 2), span]
                when(two, lambda: received(double, coarse_recv.at[1, j], mate).wait_recv())
                when(jnp.logical_not(two), lambda: received(single, coarse_recv.at[1, j], mate).wait_recv())

        top = part(q_vmem[:, columns(h)], h, early, lambda slot, b: bias[slot, b : b + 1, :])
        return top, *weigh(h, early, top)

    def arrive_late(g):
        first, _ = fine[min(g, last)]
        near = heads_of(3 - odd, g, True)
        when(
            jnp.where(odd == 1, d + 2 < n, d - 2 >= 0),
            lambda: received(near, pair_recv.at[g], pair).wait_recv(),
        )
        down, up = d - 8 >= 0, d + 8 < n
        if first < lent:
            down = jnp.logical_and(down, jnp.logical_not(high))
            up = jnp.logical_and(up, jnp.logical_not(low))
        one = jnp.logical_xor(down, up)
        when(one, lambda: received(heads_of(6, g, True), far_recv.at[g], mate).wait_recv())
        if n > 16:
            both_far = heads_of(pl.ds(6, 2), g, True)
            two = jnp.logical_and(down, up)
            when(two, lambda: received(both_far, far_recv.at[g], mate).wait_recv())

    def attend_late(h, lacking, state, values_here=None):
        top_early, total_early, numerator_early = state

        def mask(slot, b):
            return bias[slot, b : b + 1, :] + jnp.where(slot == lacking, MASKED, 0.0)

        top = jnp.maximum(top_early, part(q_vmem[:, columns(h)], h, late, mask))
        shrink = jnp.exp2((top_early - top) * C_EXP)
        total, numerator = weigh(h, late, top, values_here)
        return top, total + total_early * shrink, numerator + numerator_early * shrink

    def one_head(h, state):
        following = attend_early(h + 1)
        for g, (first, size) in enumerate(fine[:last]):

            @pl.when(h == first)
            def _():
                arrive_late(g)

        borrowed = jnp.logical_and(lends, h < lent)
        top, total, numerator = attend_late(h, jnp.where(borrowed, missing, -1), state)

        @pl.when(jnp.logical_not(borrowed))
        def _():
            out_ref[:, columns(h)] = (numerator / total).astype(out_ref.dtype)

        @pl.when(borrowed)
        def _():
            @pl.when(h == 0)
            def _():
                back_copy((0, lent)).wait_recv()
                stats_copy().wait_recv()

            stats = given_stats[...]
            top_given = jnp.sum(jnp.where(lane == h, stats, 0.0), axis=1, keepdims=True)
            total_given = jnp.sum(jnp.where(lane == h + lent, stats, 0.0), axis=1, keepdims=True)
            top_all = jnp.maximum(top, top_given)
            here = jnp.exp2((top - top_all) * C_EXP)
            there = jnp.exp2((top_given - top_all) * C_EXP)
            joined = numerator * here + given[h].astype(jnp.float32) * there
            out_ref[:, columns(h)] = (joined / (total * here + total_given * there)).astype(out_ref.dtype)

        return following

    def wait_sends():
        for index, src, dst, target, condition in (own_up, own_down, own_pair, own_mate, pass_pair, hand_on):
            when(condition, lambda: sent(index, src, target, 0).wait_send())
        for (index, src, dst, target, condition), short in (
            (pass_up, serves_high), (pass_down, serves_low)
        ):
            for skipped, met in ((0, jnp.logical_not(short)), (lent, short)):
                when(
                    jnp.logical_and(condition, met),
                    lambda: sent(index, src, target, skipped).wait_send(),
                )

        @pl.when(lends)
        def _():
            for c in lend_copies():
                c.wait_send()

        @pl.when(serves)
        def _():
            back_copy((0, lent)).wait_send()
            stats_copy().wait_send()

    state = lax.fori_loop(0, heads - 1, one_head, attend_early(jnp.int32(0)))
    arrive_late(last)
    final = jnp.int32(heads - 1)

    def values_here():
        wait_sends()
        arrive_late(last + 1)

    _, total, numerator = attend_late(final, -1, state, values_here)
    out_ref[:, columns(final)] = (numerator / total).astype(out_ref.dtype)


def per_device(queries, keys, values, kept_blocks):
    n = lax.axis_size("blk")
    rows, features = queries.shape
    heads = features // DH
    slots = len(OFFSETS)
    lent = min(LENT, heads)
    coarse, fine = len(spans(heads, ())), len(spans(heads, TAIL)) + 1
    inputs = [
        pltpu.with_memory_space_constraint(x, pltpu.HBM) for x in (kept_blocks, queries, keys, values)
    ]
    return pl.pallas_call(
        functools.partial(kernel, n, heads, lent),
        out_shape=jax.ShapeDtypeStruct((rows, features), jnp.bfloat16),
        in_specs=[pl.BlockSpec(memory_space=pltpu.HBM)] * 4,
        out_specs=pl.BlockSpec(memory_space=pltpu.VMEM),
        scratch_shapes=[
            pltpu.VMEM((slots, heads, 2, rows, DH), jnp.bfloat16),
            pltpu.SMEM(kept_blocks.shape, jnp.int32),
            pltpu.VMEM((rows, features), jnp.bfloat16),
            pltpu.VMEM((6, rows, rows), jnp.float32),
            pltpu.VMEM((slots, rows // BLOCK, rows), jnp.float32),
            pltpu.VMEM((rows, lent * DH), jnp.bfloat16),
            pltpu.VMEM((rows // BLOCK, rows), jnp.float32),
            pltpu.VMEM((lent, rows, DH), jnp.bfloat16),
            pltpu.VMEM((rows, DH), jnp.float32),
            pltpu.VMEM((lent, rows, DH), jnp.bfloat16),
            pltpu.VMEM((rows, DH), jnp.float32),
            pltpu.SemaphoreType.DMA((coarse,)),
            pltpu.SemaphoreType.DMA,
            pltpu.SemaphoreType.DMA,
            pltpu.SemaphoreType.DMA((8,)),
            pltpu.SemaphoreType.DMA((2, coarse)),
            pltpu.SemaphoreType.DMA((fine + coarse,)),
            pltpu.SemaphoreType.DMA((fine,)),
            pltpu.SemaphoreType.DMA((4,)),
            pltpu.SemaphoreType.DMA((4,)),
        ],
        compiler_params=pltpu.CompilerParams(
            collective_id=0, has_side_effects=True, vmem_limit_bytes=40 * 2**20
        ),
    )(*inputs)


def solution(mesh):
    placed = P(("clip", "blk"), None)
    return jax.shard_map(
        per_device, mesh=mesh, in_specs=(placed,) * 4, out_specs=placed, check_vma=False
    )
```

```python
import functools
import math

import jax
import jax.numpy as jnp
from jax import lax
from jax.experimental import pallas as pl
from jax.experimental.pallas import tpu as pltpu
from jax.sharding import PartitionSpec as P

DH = 128
BLOCK = 128
GROUP = 4
TAIL = (2, 2, 1, 1, 1, 1)
LENT = 4
HELD = 12

OFFSETS = (1, -1, 2, -2, 4, -4, 8, -8, 0)
OWN = 8
MASKED = -1e30
C_EXP = math.log2(math.e) / math.sqrt(DH)


def spans(heads, tail):
    sizes = [GROUP] * ((heads - sum(tail)) // GROUP) + list(tail)
    return [(sum(sizes[:i]), size) for i, size in enumerate(sizes)]


def kernel(
    n, heads, lent, kept_hbm, q_hbm, k_hbm, v_hbm, out_ref,
    kv, kept_ref, q_vmem, scores, bias, guest_q, guest_bias, back, back_stats, given, given_stats,
    local_sem, kept_sem, q_sem, send_sem, coarse_recv, late_recv, lend_send, lend_recv,
):
    rows = kv.shape[-2]
    local_blocks = rows // BLOCK
    d = lax.axis_index("blk")
    r = lax.rem(d, 4)
    upper = r // 2
    odd = lax.rem(r, 2)
    straight = odd == upper
    crossed = odd != upper

    pair = d + 2 - 4 * upper
    mate = d + 1 - 2 * odd
    has_up = d + 4 < n
    has_down = d - 4 >= 0
    both = jnp.logical_and(has_up, has_down)

    low, high = d < 4, d + 4 >= n
    serves_low = jnp.logical_and(d >= 4, d < 8)
    serves_high = jnp.logical_and(d + 4 < n, d + 8 >= n)
    lends = jnp.logical_or(low, high)
    serves = jnp.logical_or(serves_low, serves_high)
    server = jnp.where(low, d + 4, d - 4)
    guest = jnp.where(serves_low, d - 4, d + 4)
    missing = jnp.where(low, 6, 7)
    served = jnp.where(serves_low, 4, 5)

    coarse = spans(heads, ())
    fine = spans(heads, TAIL)
    lag = HELD // GROUP

    def columns(h):
        return pl.ds(pl.multiple_of(h * DH, DH), DH)

    loads = [coarse[0], (coarse[0][1], heads - coarse[0][1])]

    def load(j):
        first, size = loads[j]

        @pl.loop(first, first + size)
        def _(h):
            for i, hbm in ((0, k_hbm), (1, v_hbm)):
                pltpu.make_async_copy(hbm.at[:, columns(h)], kv.at[OWN, h, i], local_sem.at[j]).start()

    def loaded(j):
        group = kv.at[OWN, pl.ds(*loads[j])]
        pltpu.make_async_copy(group, group, local_sem.at[j]).wait()

    def sem_of(kind, g):
        if kind == "far":
            return late_recv.at[g]
        if kind in ("z", "mate"):
            return coarse_recv.at[("z", "mate").index(kind), g]
        first = fine[min(g, last)][0]
        j = max(j for j, span in enumerate(coarse) if span[0] <= first)
        handed = crossed if kind == "own" else straight
        return late_recv.at[jnp.where(handed, last + 2 + j, g)]

    last = len(fine) - 1

    def heads_of(slot, g, is_fine):
        if is_fine and g >= last:
            return kv.at[slot, fine[last][0], g - last]
        return kv.at[slot, pl.ds(*(fine[g] if is_fine else coarse[g]))]

    def flow(index, src_slot, dst_slot, target, g, kind):
        is_fine = kind not in ("z", "mate")
        return pltpu.make_async_remote_copy(
            src_ref=heads_of(src_slot, g, is_fine),
            dst_ref=heads_of(dst_slot, g, is_fine),
            send_sem=send_sem.at[index],
            recv_sem=sem_of(kind, g),
            device_id={"blk": target},
            device_id_type=pl.DeviceIdType.MESH,
        )

    def received(group, sem, sender):
        return pltpu.make_async_remote_copy(
            src_ref=group,
            dst_ref=group,
            send_sem=send_sem.at[0],
            recv_sem=sem,
            device_id={"blk": sender},
            device_id_type=pl.DeviceIdType.MESH,
        )

    def sent(index, src_slot, target, skipped):
        some = pl.ds(skipped, heads - skipped)
        return pltpu.make_async_remote_copy(
            src_ref=kv.at[src_slot, some],
            dst_ref=kv.at[src_slot, some],
            send_sem=send_sem.at[index],
            recv_sem=coarse_recv.at[0, 0],
            device_id={"blk": target},
            device_id_type=pl.DeviceIdType.MESH,
        )

    own_up = (0, OWN, 5, d + 4, has_up)
    own_down = (1, OWN, 4, d - 4, has_down)
    own_pair = (2, OWN, 3 - upper, pair, None)
    own_mate = (3, OWN, 1 - odd, mate, None)
    pass_up = (4, 5, 7, d + 4, both)
    pass_down = (5, 4, 6, d - 4, both)
    pass_pair = (6, 4 + upper, 2 + upper, pair, jnp.where(upper == 1, d - 4 >= 0, d + 4 < n))
    hand_on = (7, 2 + odd, odd, mate, jnp.where(odd == 1, d - 2 >= 0, d + 2 < n))

    def remote(src, dst, sends, receives, target):
        return pltpu.make_async_remote_copy(
            src_ref=src,
            dst_ref=dst,
            send_sem=sends,
            recv_sem=receives,
            device_id={"blk": target},
            device_id_type=pl.DeviceIdType.MESH,
        )

    def lend_copies():
        return (
            remote(bias.at[missing], guest_bias, lend_send.at[0], lend_recv.at[0], server),
            remote(q_vmem.at[:, pl.ds(0, lent * DH)], guest_q, lend_send.at[1], lend_recv.at[1], server),
        )

    def back_copy(span):
        return remote(back.at[pl.ds(*span)], given.at[pl.ds(*span)], lend_send.at[0], lend_recv.at[0], guest)

    def stats_copy():
        return remote(back_stats, given_stats, lend_send.at[1], lend_recv.at[1], guest)

    def when(condition, action):
        if condition is None:
            action()
        else:
            pl.when(condition)(action)

    def start(a_flow, g, kind):
        *rest, condition = a_flow
        when(condition, lambda: flow(*rest, g, kind).start())

    def within(j):
        first, size = coarse[j]
        groups = [g for g, (start, _) in enumerate(fine) if first <= start < first + size]
        return groups + [last + 1] * (last in groups)

    barrier = pltpu.get_barrier_semaphore()
    for target, condition in ((d + 4, has_up), (d - 4, has_down), (pair, None), (mate, None)):
        when(
            condition,
            lambda: pl.semaphore_signal(
                barrier, inc=1, device_id={"blk": target}, device_id_type=pl.DeviceIdType.MESH
            ),
        )
    load(0)
    pl.semaphore_wait(barrier, 2 + has_up.astype(jnp.int32) + has_down.astype(jnp.int32))

    def send_own(j):
        if j < 2:
            loaded(j)
        start(own_up, j, "z")
        start(own_down, j, "z")
        if coarse[j][0] < HELD:
            for g in within(j):
                start(own_pair, g, "own")
        else:

            @pl.when(crossed)
            def _():
                for g in within(j):
                    start(own_pair, g, "own")

        start(own_mate, j, "mate")
        if j == 0:
            load(1)

    send_own(0)

    q_copy = pltpu.make_async_copy(q_hbm, q_vmem, q_sem)
    q_copy.start()
    kept_copy = pltpu.make_async_copy(kept_hbm, kept_ref, kept_sem)
    kept_copy.start()

    def prepare():
        kept_copy.wait()
        for query_slot in range(local_blocks):
            kept = [kept_ref[query_slot, j] for j in range(kept_ref.shape[1])]
            for slot, offset in enumerate(OFFSETS):
                inside = jnp.logical_and(d + offset >= 0, d + offset < n)
                for key_slot in range(local_blocks):
                    block = (d + offset) * local_blocks + key_slot
                    allowed = functools.reduce(jnp.logical_or, [j == block for j in kept])
                    bias[slot, pl.ds(query_slot, 1), pl.ds(key_slot * BLOCK, BLOCK)] = jnp.full(
                        (1, BLOCK), jnp.where(jnp.logical_and(allowed, inside), 0.0, MASKED), jnp.float32
                    )
        q_copy.wait()

    prepare()

    @pl.when(lends)
    def _():
        for c in lend_copies():
            c.start()

    for j in range(1, len(coarse)):
        send_own(j)

    for slot, offset in enumerate(OFFSETS[:OWN]):
        source = d + offset

        @pl.when(jnp.logical_or(source < 0, source >= n))
        def _():
            @pl.loop(0, heads)
            def _(h):
                kv[slot, h] = jnp.zeros(kv.shape[2:], kv.dtype)

    @pl.when(lends)
    def _():
        @pl.loop(0, lent)
        def _(h):
            kv[missing, h] = jnp.zeros(kv.shape[2:], kv.dtype)

    @pl.when(serves)
    def _():
        back_stats[...] = jnp.zeros(back_stats.shape, back_stats.dtype)
        for c in lend_copies():
            c.wait_recv()

    def part(q, h, slots, mask):
        tops = [None] * local_blocks
        for i, slot in enumerate(slots):
            s = lax.dot_general(
                q, kv[slot, h, 0], (((1,), (1,)), ((), ())), preferred_element_type=jnp.float32
            )
            for b in range(local_blocks):
                masked = s[b * BLOCK : (b + 1) * BLOCK] + mask(slot, b)
                scores[i, b * BLOCK : (b + 1) * BLOCK] = masked
                tops[b] = masked if tops[b] is None else jnp.maximum(tops[b], masked)
        return jnp.concatenate([jnp.max(t, axis=1, keepdims=True) for t in tops], axis=0)

    def weigh(h, slots, top, values_here=None):
        sums = None
        numerator = None
        kept = []
        for i, slot in enumerate(slots):
            weight = jnp.exp2((scores[i] - top) * C_EXP)
            sums = weight if sums is None else sums + weight
            kept.append(weight.astype(jnp.bfloat16))
            if values_here is None:
                term = jnp.dot(kept[i], kv[slot, h, 1], preferred_element_type=jnp.float32)
                numerator = term if numerator is None else numerator + term
        total = jnp.sum(sums, axis=1, keepdims=True)
        if values_here is not None:
            values_here()
            for i, slot in enumerate(slots):
                term = jnp.dot(kept[i], kv[slot, h, 1], preferred_element_type=jnp.float32)
                numerator = term if numerator is None else numerator + term
        return total, numerator

    lane = lax.broadcasted_iota(jnp.int32, back_stats.shape, 1)

    def serve(h):
        top = part(guest_q[:, columns(h)], h, (served,), lambda slot, b: guest_bias[b : b + 1, :])
        total, numerator = weigh(h, (served,), top)
        back[h] = numerator.astype(back.dtype)
        stats = jnp.where(lane == h, top, back_stats[...])
        back_stats[...] = jnp.where(lane == h + lent, total, stats)

    def hand_over(j):
        group = kv.at[2 + odd, pl.ds(*coarse[j])]
        when(hand_on[-1], lambda: received(group, late_recv.at[last + 2 + j], pair).wait_recv())
        start(hand_on, j, "mate")

    for j, span in enumerate(coarse):
        single, double = kv.at[jnp.where(has_up, 4, 5), pl.ds(*span)], kv.at[pl.ds(4, 2), pl.ds(*span)]
        when(both, lambda: received(double, coarse_recv.at[0, j], mate).wait_recv())
        when(jnp.logical_not(both), lambda: received(single, coarse_recv.at[0, j], mate).wait_recv())
        for g in within(j):
            start(pass_pair, g, "pass")
        if span[0] < lent:
            for a_flow, serving in ((pass_up, serves_high), (pass_down, serves_low)):

                @pl.when(jnp.logical_not(serving))
                def _():
                    for g in within(j):
                        start(a_flow, g, "far")

            @pl.when(serves)
            def _():
                pl.loop(span[0], sum(span))(serve)
                back_copy(span).start()
                if sum(span) == lent:
                    stats_copy().start()
        else:
            for g in within(j):
                start(pass_up, g, "far")
                start(pass_down, g, "far")

        @pl.when(straight)
        def _():
            hand_over(j)

        if j >= lag:

            @pl.when(crossed)
            def _():
                hand_over(j - lag)

    @pl.when(straight)
    def _():
        for j, (first, _) in enumerate(coarse):
            if first >= HELD:
                for g in within(j):
                    start(own_pair, g, "own")

    early = (OWN, 4, 5, 0, 1, 2 + odd)
    far = (6, 7) if n > 16 else (jnp.where(d - 8 >= 0, 7, 6),)
    late = (3 - odd, *far)

    def attend_early(h):
        for j, (first, _) in enumerate(coarse):

            @pl.when(h == first)
            def _():
                if 1 <= j <= lag:

                    @pl.when(crossed)
                    def _():
                        hand_over(len(coarse) - lag - 1 + j)

                span = pl.ds(*coarse[j])
                two = jnp.where(odd == 1, d + 1 < n, d - 1 >= 0)
                single, double = kv.at[odd, span], kv.at[pl.ds(0, 2), span]
                when(two, lambda: received(double, coarse_recv.at[1, j], mate).wait_recv())
                when(jnp.logical_not(two), lambda: received(single, coarse_recv.at[1, j], mate).wait_recv())

        top = part(q_vmem[:, columns(h)], h, early, lambda slot, b: bias[slot, b : b + 1, :])
        return top, *weigh(h, early, top)

    def arrive_late(g):
        first, _ = fine[min(g, last)]
        near = jnp.where(odd == 1, d + 2 < n, d - 2 >= 0)
        down, up = d - 8 >= 0, d + 8 < n
        if first < lent:
            down = jnp.logical_and(down, jnp.logical_not(high))
            up = jnp.logical_and(up, jnp.logical_not(low))
        arriving = near.astype(jnp.int32) + down.astype(jnp.int32) + up.astype(jnp.int32)
        for count in range(1, 4 if n > 16 else 3):
            group = heads_of(pl.ds(5, count), g, True)
            when(arriving == count, lambda: received(group, late_recv.at[g], mate).wait_recv())

    def attend_late(h, lacking, state, values_here=None):
        top_early, total_early, numerator_early = state

        def mask(slot, b):
            return bias[slot, b : b + 1, :] + jnp.where(slot == lacking, MASKED, 0.0)

        top = jnp.maximum(top_early, part(q_vmem[:, columns(h)], h, late, mask))
        shrink = jnp.exp2((top_early - top) * C_EXP)
        total, numerator = weigh(h, late, top, values_here)
        return top, total + total_early * shrink, numerator + numerator_early * shrink

    def one_head(h, state):
        following = attend_early(h + 1)
        for g, (first, size) in enumerate(fine[:last]):

            @pl.when(h == first)
            def _():
                arrive_late(g)

        borrowed = jnp.logical_and(lends, h < lent)
        top, total, numerator = attend_late(h, jnp.where(borrowed, missing, -1), state)

        @pl.when(jnp.logical_not(borrowed))
        def _():
            out_ref[:, columns(h)] = (numerator / total).astype(out_ref.dtype)

        @pl.when(borrowed)
        def _():
            @pl.when(h == 0)
            def _():
                back_copy((0, lent)).wait_recv()
                stats_copy().wait_recv()

            stats = given_stats[...]
            top_given = jnp.sum(jnp.where(lane == h, stats, 0.0), axis=1, keepdims=True)
            total_given = jnp.sum(jnp.where(lane == h + lent, stats, 0.0), axis=1, keepdims=True)
            top_all = jnp.maximum(top, top_given)
            here = jnp.exp2((top - top_all) * C_EXP)
            there = jnp.exp2((top_given - top_all) * C_EXP)
            joined = numerator * here + given[h].astype(jnp.float32) * there
            out_ref[:, columns(h)] = (joined / (total * here + total_given * there)).astype(out_ref.dtype)

        return following

    def wait_sends():
        for index, src, dst, target, condition in (own_up, own_down, own_pair, own_mate, pass_pair, hand_on):
            when(condition, lambda: sent(index, src, target, 0).wait_send())
        for (index, src, dst, target, condition), short in (
            (pass_up, serves_high), (pass_down, serves_low)
        ):
            for skipped, met in ((0, jnp.logical_not(short)), (lent, short)):
                when(
                    jnp.logical_and(condition, met),
                    lambda: sent(index, src, target, skipped).wait_send(),
                )

        @pl.when(lends)
        def _():
            for c in lend_copies():
                c.wait_send()

        @pl.when(serves)
        def _():
            back_copy((0, lent)).wait_send()
            stats_copy().wait_send()

    state = lax.fori_loop(0, heads - 1, one_head, attend_early(jnp.int32(0)))
    arrive_late(last)
    final = jnp.int32(heads - 1)

    def values_here():
        wait_sends()
        arrive_late(last + 1)

    _, total, numerator = attend_late(final, -1, state, values_here)
    out_ref[:, columns(final)] = (numerator / total).astype(out_ref.dtype)


def per_device(queries, keys, values, kept_blocks):
    n = lax.axis_size("blk")
    rows, features = queries.shape
    heads = features // DH
    slots = len(OFFSETS)
    lent = min(LENT, heads)
    coarse, fine = len(spans(heads, ())), len(spans(heads, TAIL)) + 1
    inputs = [
        pltpu.with_memory_space_constraint(x, pltpu.HBM) for x in (kept_blocks, queries, keys, values)
    ]
    return pl.pallas_call(
        functools.partial(kernel, n, heads, lent),
        out_shape=jax.ShapeDtypeStruct((rows, features), jnp.bfloat16),
        in_specs=[pl.BlockSpec(memory_space=pltpu.HBM)] * 4,
        out_specs=pl.BlockSpec(memory_space=pltpu.VMEM),
        scratch_shapes=[
            pltpu.VMEM((slots, heads, 2, rows, DH), jnp.bfloat16),
            pltpu.SMEM(kept_blocks.shape, jnp.int32),
            pltpu.VMEM((rows, features), jnp.bfloat16),
            pltpu.VMEM((6, rows, rows), jnp.float32),
            pltpu.VMEM((slots, rows // BLOCK, rows), jnp.float32),
            pltpu.VMEM((rows, lent * DH), jnp.bfloat16),
            pltpu.VMEM((rows // BLOCK, rows), jnp.float32),
            pltpu.VMEM((lent, rows, DH), jnp.bfloat16),
            pltpu.VMEM((rows, DH), jnp.float32),
            pltpu.VMEM((lent, rows, DH), jnp.bfloat16),
            pltpu.VMEM((rows, DH), jnp.float32),
            pltpu.SemaphoreType.DMA((2,)),
            pltpu.SemaphoreType.DMA,
            pltpu.SemaphoreType.DMA,
            pltpu.SemaphoreType.DMA((8,)),
            pltpu.SemaphoreType.DMA((2, coarse)),
            pltpu.SemaphoreType.DMA((fine + coarse,)),
            pltpu.SemaphoreType.DMA((2,)),
            pltpu.SemaphoreType.DMA((2,)),
        ],
        compiler_params=pltpu.CompilerParams(
            collective_id=0, has_side_effects=True, vmem_limit_bytes=40 * 2**20
        ),
    )(*inputs)


def solution(mesh):
    placed = P(("clip", "blk"), None)
    return jax.shard_map(
        per_device, mesh=mesh, in_specs=(placed,) * 4, out_specs=placed, check_vma=False
    )
```

```python
import functools
import math

import jax
import jax.numpy as jnp
from jax import lax
from jax.experimental import pallas as pl
from jax.experimental.pallas import tpu as pltpu
from jax.sharding import PartitionSpec as P

DH = 128
BLOCK = 128
GROUP = 4
TAIL = (2, 2, 1, 1, 1, 1)
LENT = 4
HELD = 8

OFFSETS = (1, -1, 2, -2, 4, -4, 8, -8, 0)
OWN = 8
MASKED = -1e30
C_EXP = math.log2(math.e) / math.sqrt(DH)


def spans(heads, tail):
    sizes = [GROUP] * ((heads - sum(tail)) // GROUP) + list(tail)
    return [(sum(sizes[:i]), size) for i, size in enumerate(sizes)]


def kernel(
    n, heads, lent, kept_hbm, q_hbm, k_hbm, v_hbm, out_ref,
    kv, kept_ref, q_vmem, scores, bias, guest_q, guest_bias, back, back_stats, given, given_stats,
    local_sem, kept_sem, q_sem, send_sem, coarse_recv, late_recv, lend_send, lend_recv,
):
    rows = kv.shape[-2]
    local_blocks = rows // BLOCK
    d = lax.axis_index("blk")
    r = lax.rem(d, 4)
    upper = r // 2
    odd = lax.rem(r, 2)
    straight = odd == upper
    crossed = odd != upper

    pair = d + 2 - 4 * upper
    mate = d + 1 - 2 * odd
    has_up = d + 4 < n
    has_down = d - 4 >= 0
    both = jnp.logical_and(has_up, has_down)

    low, high = d < 4, d + 4 >= n
    serves_low = jnp.logical_and(d >= 4, d < 8)
    serves_high = jnp.logical_and(d + 4 < n, d + 8 >= n)
    lends = jnp.logical_or(low, high)
    serves = jnp.logical_or(serves_low, serves_high)
    server = jnp.where(low, d + 4, d - 4)
    guest = jnp.where(serves_low, d - 4, d + 4)
    missing = jnp.where(low, 6, 7)
    served = jnp.where(serves_low, 4, 5)

    coarse = spans(heads, ())
    fine = spans(heads, TAIL)
    lag = HELD // GROUP

    def columns(h):
        return pl.ds(pl.multiple_of(h * DH, DH), DH)

    loads = [coarse[0], (coarse[0][1], heads - coarse[0][1])]

    def load(j):
        first, size = loads[j]

        @pl.loop(first, first + size)
        def _(h):
            for i, hbm in ((0, k_hbm), (1, v_hbm)):
                pltpu.make_async_copy(hbm.at[:, columns(h)], kv.at[OWN, h, i], local_sem.at[j]).start()

    def loaded(j):
        group = kv.at[OWN, pl.ds(*loads[j])]
        pltpu.make_async_copy(group, group, local_sem.at[j]).wait()

    def sem_of(kind, g):
        if kind == "far":
            return late_recv.at[g]
        if kind in ("z", "mate"):
            return coarse_recv.at[("z", "mate").index(kind), g]
        first = fine[min(g, last)][0]
        j = max(j for j, span in enumerate(coarse) if span[0] <= first)
        handed = crossed if kind == "own" else straight
        return late_recv.at[jnp.where(handed, last + 2 + j, g)]

    last = len(fine) - 1

    def heads_of(slot, g, is_fine):
        if is_fine and g >= last:
            return kv.at[slot, fine[last][0], g - last]
        return kv.at[slot, pl.ds(*(fine[g] if is_fine else coarse[g]))]

    def flow(index, src_slot, dst_slot, target, g, kind):
        is_fine = kind not in ("z", "mate")
        return pltpu.make_async_remote_copy(
            src_ref=heads_of(src_slot, g, is_fine),
            dst_ref=heads_of(dst_slot, g, is_fine),
            send_sem=send_sem.at[index],
            recv_sem=sem_of(kind, g),
            device_id={"blk": target},
            device_id_type=pl.DeviceIdType.MESH,
        )

    def received(group, sem, sender):
        return pltpu.make_async_remote_copy(
            src_ref=group,
            dst_ref=group,
            send_sem=send_sem.at[0],
            recv_sem=sem,
            device_id={"blk": sender},
            device_id_type=pl.DeviceIdType.MESH,
        )

    def sent(index, src_slot, target, skipped):
        some = pl.ds(skipped, heads - skipped)
        return pltpu.make_async_remote_copy(
            src_ref=kv.at[src_slot, some],
            dst_ref=kv.at[src_slot, some],
            send_sem=send_sem.at[index],
            recv_sem=coarse_recv.at[0, 0],
            device_id={"blk": target},
            device_id_type=pl.DeviceIdType.MESH,
        )

    own_up = (0, OWN, 5, d + 4, has_up)
    own_down = (1, OWN, 4, d - 4, has_down)
    own_pair = (2, OWN, 3 - upper, pair, None)
    own_mate = (3, OWN, 1 - odd, mate, None)
    pass_up = (4, 5, 7, d + 4, both)
    pass_down = (5, 4, 6, d - 4, both)
    pass_pair = (6, 4 + upper, 2 + upper, pair, jnp.where(upper == 1, d - 4 >= 0, d + 4 < n))
    hand_on = (7, 2 + odd, odd, mate, jnp.where(odd == 1, d - 2 >= 0, d + 2 < n))

    def remote(src, dst, sends, receives, target):
        return pltpu.make_async_remote_copy(
            src_ref=src,
            dst_ref=dst,
            send_sem=sends,
            recv_sem=receives,
            device_id={"blk": target},
            device_id_type=pl.DeviceIdType.MESH,
        )

    def lend_copies():
        return (
            remote(bias.at[missing], guest_bias, lend_send.at[0], lend_recv.at[0], server),
            remote(q_vmem.at[:, pl.ds(0, lent * DH)], guest_q, lend_send.at[1], lend_recv.at[1], server),
        )

    def back_copy(span):
        return remote(back.at[pl.ds(*span)], given.at[pl.ds(*span)], lend_send.at[0], lend_recv.at[0], guest)

    def stats_copy():
        return remote(back_stats, given_stats, lend_send.at[1], lend_recv.at[1], guest)

    def when(condition, action):
        if condition is None:
            action()
        else:
            pl.when(condition)(action)

    def start(a_flow, g, kind):
        *rest, condition = a_flow
        when(condition, lambda: flow(*rest, g, kind).start())

    def within(j):
        first, size = coarse[j]
        groups = [g for g, (start, _) in enumerate(fine) if first <= start < first + size]
        return groups + [last + 1] * (last in groups)

    barrier = pltpu.get_barrier_semaphore()
    for target, condition in ((d + 4, has_up), (d - 4, has_down), (pair, None), (mate, None)):
        when(
            condition,
            lambda: pl.semaphore_signal(
                barrier, inc=1, device_id={"blk": target}, device_id_type=pl.DeviceIdType.MESH
            ),
        )
    load(0)
    pl.semaphore_wait(barrier, 2 + has_up.astype(jnp.int32) + has_down.astype(jnp.int32))

    def send_own(j):
        if j < 2:
            loaded(j)
        start(own_up, j, "z")
        start(own_down, j, "z")
        if coarse[j][0] < HELD:
            for g in within(j):
                start(own_pair, g, "own")
        else:

            @pl.when(crossed)
            def _():
                for g in within(j):
                    start(own_pair, g, "own")

        start(own_mate, j, "mate")
        if j == 0:
            load(1)

    send_own(0)

    q_copy = pltpu.make_async_copy(q_hbm, q_vmem, q_sem)
    q_copy.start()
    kept_copy = pltpu.make_async_copy(kept_hbm, kept_ref, kept_sem)
    kept_copy.start()

    def prepare():
        kept_copy.wait()
        for query_slot in range(local_blocks):
            kept = [kept_ref[query_slot, j] for j in range(kept_ref.shape[1])]
            for slot, offset in enumerate(OFFSETS):
                inside = jnp.logical_and(d + offset >= 0, d + offset < n)
                for key_slot in range(local_blocks):
                    block = (d + offset) * local_blocks + key_slot
                    allowed = functools.reduce(jnp.logical_or, [j == block for j in kept])
                    bias[slot, pl.ds(query_slot, 1), pl.ds(key_slot * BLOCK, BLOCK)] = jnp.full(
                        (1, BLOCK), jnp.where(jnp.logical_and(allowed, inside), 0.0, MASKED), jnp.float32
                    )
        q_copy.wait()

    prepare()

    @pl.when(lends)
    def _():
        for c in lend_copies():
            c.start()

    for j in range(1, len(coarse)):
        send_own(j)

    for slot, offset in enumerate(OFFSETS[:OWN]):
        source = d + offset

        @pl.when(jnp.logical_or(source < 0, source >= n))
        def _():
            @pl.loop(0, heads)
            def _(h):
                kv[slot, h] = jnp.zeros(kv.shape[2:], kv.dtype)

    @pl.when(lends)
    def _():
        @pl.loop(0, lent)
        def _(h):
            kv[missing, h] = jnp.zeros(kv.shape[2:], kv.dtype)

    @pl.when(serves)
    def _():
        back_stats[...] = jnp.zeros(back_stats.shape, back_stats.dtype)
        for c in lend_copies():
            c.wait_recv()

    def part(q, h, slots, mask):
        tops = [None] * local_blocks
        for i, slot in enumerate(slots):
            s = lax.dot_general(
                q, kv[slot, h, 0], (((1,), (1,)), ((), ())), preferred_element_type=jnp.float32
            )
            for b in range(local_blocks):
                masked = s[b * BLOCK : (b + 1) * BLOCK] + mask(slot, b)
                scores[i, b * BLOCK : (b + 1) * BLOCK] = masked
                tops[b] = masked if tops[b] is None else jnp.maximum(tops[b], masked)
        return jnp.concatenate([jnp.max(t, axis=1, keepdims=True) for t in tops], axis=0)

    def weigh(h, slots, top, values_here=None):
        sums = None
        numerator = None
        kept = []
        for i, slot in enumerate(slots):
            weight = jnp.exp2((scores[i] - top) * C_EXP)
            sums = weight if sums is None else sums + weight
            kept.append(weight.astype(jnp.bfloat16))
            if values_here is None:
                term = jnp.dot(kept[i], kv[slot, h, 1], preferred_element_type=jnp.float32)
                numerator = term if numerator is None else numerator + term
        total = jnp.sum(sums, axis=1, keepdims=True)
        if values_here is not None:
            values_here()
            for i, slot in enumerate(slots):
                term = jnp.dot(kept[i], kv[slot, h, 1], preferred_element_type=jnp.float32)
                numerator = term if numerator is None else numerator + term
        return total, numerator

    lane = lax.broadcasted_iota(jnp.int32, back_stats.shape, 1)

    def serve(h):
        top = part(guest_q[:, columns(h)], h, (served,), lambda slot, b: guest_bias[b : b + 1, :])
        total, numerator = weigh(h, (served,), top)
        back[h] = numerator.astype(back.dtype)
        stats = jnp.where(lane == h, top, back_stats[...])
        back_stats[...] = jnp.where(lane == h + lent, total, stats)

    def hand_over(j):
        group = kv.at[2 + odd, pl.ds(*coarse[j])]
        when(hand_on[-1], lambda: received(group, late_recv.at[last + 2 + j], pair).wait_recv())
        start(hand_on, j, "mate")

    for j, span in enumerate(coarse):
        single, double = kv.at[jnp.where(has_up, 4, 5), pl.ds(*span)], kv.at[pl.ds(4, 2), pl.ds(*span)]
        when(both, lambda: received(double, coarse_recv.at[0, j], mate).wait_recv())
        when(jnp.logical_not(both), lambda: received(single, coarse_recv.at[0, j], mate).wait_recv())
        for g in within(j):
            start(pass_pair, g, "pass")
        if span[0] < lent:
            for a_flow, serving in ((pass_up, serves_high), (pass_down, serves_low)):

                @pl.when(jnp.logical_not(serving))
                def _():
                    for g in within(j):
                        start(a_flow, g, "far")

            @pl.when(serves)
            def _():
                pl.loop(span[0], sum(span))(serve)
                back_copy(span).start()
                if sum(span) == lent:
                    stats_copy().start()
        else:
            for g in within(j):
                start(pass_up, g, "far")
                start(pass_down, g, "far")

        @pl.when(straight)
        def _():
            hand_over(j)

        if j >= lag:

            @pl.when(crossed)
            def _():
                hand_over(j - lag)

    @pl.when(straight)
    def _():
        for j, (first, _) in enumerate(coarse):
            if first >= HELD:
                for g in within(j):
                    start(own_pair, g, "own")

    early = (OWN, 4, 5, 0, 1, 2 + odd)
    far = (6, 7) if n > 16 else (jnp.where(d - 8 >= 0, 7, 6),)
    late = (3 - odd, *far)

    def attend_early(h):
        for j, (first, _) in enumerate(coarse):

            @pl.when(h == first)
            def _():
                if 1 <= j <= lag:

                    @pl.when(crossed)
                    def _():
                        hand_over(len(coarse) - lag - 1 + j)

                span = pl.ds(*coarse[j])
                two = jnp.where(odd == 1, d + 1 < n, d - 1 >= 0)
                single, double = kv.at[odd, span], kv.at[pl.ds(0, 2), span]
                when(two, lambda: received(double, coarse_recv.at[1, j], mate).wait_recv())
                when(jnp.logical_not(two), lambda: received(single, coarse_recv.at[1, j], mate).wait_recv())

        top = part(q_vmem[:, columns(h)], h, early, lambda slot, b: bias[slot, b : b + 1, :])
        return top, *weigh(h, early, top)

    def arrive_late(g):
        first, _ = fine[min(g, last)]
        near = jnp.where(odd == 1, d + 2 < n, d - 2 >= 0)
        down, up = d - 8 >= 0, d + 8 < n
        if first < lent:
            down = jnp.logical_and(down, jnp.logical_not(high))
            up = jnp.logical_and(up, jnp.logical_not(low))
        arriving = near.astype(jnp.int32) + down.astype(jnp.int32) + up.astype(jnp.int32)
        for count in range(1, 4 if n > 16 else 3):
            group = heads_of(pl.ds(5, count), g, True)
            when(arriving == count, lambda: received(group, late_recv.at[g], mate).wait_recv())

    def attend_late(h, lacking, state, values_here=None):
        top_early, total_early, numerator_early = state

        def mask(slot, b):
            return bias[slot, b : b + 1, :] + jnp.where(slot == lacking, MASKED, 0.0)

        top = jnp.maximum(top_early, part(q_vmem[:, columns(h)], h, late, mask))
        shrink = jnp.exp2((top_early - top) * C_EXP)
        total, numerator = weigh(h, late, top, values_here)
        return top, total + total_early * shrink, numerator + numerator_early * shrink

    def one_head(h, state):
        following = attend_early(h + 1)
        for g, (first, size) in enumerate(fine[:last]):

            @pl.when(h == first)
            def _():
                arrive_late(g)

        borrowed = jnp.logical_and(lends, h < lent)
        top, total, numerator = attend_late(h, jnp.where(borrowed, missing, -1), state)

        @pl.when(jnp.logical_not(borrowed))
        def _():
            out_ref[:, columns(h)] = (numerator / total).astype(out_ref.dtype)

        @pl.when(borrowed)
        def _():
            @pl.when(h == 0)
            def _():
                back_copy((0, lent)).wait_recv()
                stats_copy().wait_recv()

            stats = given_stats[...]
            top_given = jnp.sum(jnp.where(lane == h, stats, 0.0), axis=1, keepdims=True)
            total_given = jnp.sum(jnp.where(lane == h + lent, stats, 0.0), axis=1, keepdims=True)
            top_all = jnp.maximum(top, top_given)
            here = jnp.exp2((top - top_all) * C_EXP)
            there = jnp.exp2((top_given - top_all) * C_EXP)
            joined = numerator * here + given[h].astype(jnp.float32) * there
            out_ref[:, columns(h)] = (joined / (total * here + total_given * there)).astype(out_ref.dtype)

        return following

    def wait_sends():
        for index, src, dst, target, condition in (own_up, own_down, own_pair, own_mate, pass_pair, hand_on):
            when(condition, lambda: sent(index, src, target, 0).wait_send())
        for (index, src, dst, target, condition), short in (
            (pass_up, serves_high), (pass_down, serves_low)
        ):
            for skipped, met in ((0, jnp.logical_not(short)), (lent, short)):
                when(
                    jnp.logical_and(condition, met),
                    lambda: sent(index, src, target, skipped).wait_send(),
                )

        @pl.when(lends)
        def _():
            for c in lend_copies():
                c.wait_send()

        @pl.when(serves)
        def _():
            back_copy((0, lent)).wait_send()
            stats_copy().wait_send()

    state = lax.fori_loop(0, heads - 1, one_head, attend_early(jnp.int32(0)))
    arrive_late(last)
    final = jnp.int32(heads - 1)

    def values_here():
        wait_sends()
        arrive_late(last + 1)

    _, total, numerator = attend_late(final, -1, state, values_here)
    out_ref[:, columns(final)] = (numerator / total).astype(out_ref.dtype)


def per_device(queries, keys, values, kept_blocks):
    n = lax.axis_size("blk")
    rows, features = queries.shape
    heads = features // DH
    slots = len(OFFSETS)
    lent = min(LENT, heads)
    coarse, fine = len(spans(heads, ())), len(spans(heads, TAIL)) + 1
    inputs = [
        pltpu.with_memory_space_constraint(x, pltpu.HBM) for x in (kept_blocks, queries, keys, values)
    ]
    return pl.pallas_call(
        functools.partial(kernel, n, heads, lent),
        out_shape=jax.ShapeDtypeStruct((rows, features), jnp.bfloat16),
        in_specs=[pl.BlockSpec(memory_space=pltpu.HBM)] * 4,
        out_specs=pl.BlockSpec(memory_space=pltpu.VMEM),
        scratch_shapes=[
            pltpu.VMEM((slots, heads, 2, rows, DH), jnp.bfloat16),
            pltpu.SMEM(kept_blocks.shape, jnp.int32),
            pltpu.VMEM((rows, features), jnp.bfloat16),
            pltpu.VMEM((6, rows, rows), jnp.float32),
            pltpu.VMEM((slots, rows // BLOCK, rows), jnp.float32),
            pltpu.VMEM((rows, lent * DH), jnp.bfloat16),
            pltpu.VMEM((rows // BLOCK, rows), jnp.float32),
            pltpu.VMEM((lent, rows, DH), jnp.bfloat16),
            pltpu.VMEM((rows, DH), jnp.float32),
            pltpu.VMEM((lent, rows, DH), jnp.bfloat16),
            pltpu.VMEM((rows, DH), jnp.float32),
            pltpu.SemaphoreType.DMA((2,)),
            pltpu.SemaphoreType.DMA,
            pltpu.SemaphoreType.DMA,
            pltpu.SemaphoreType.DMA((8,)),
            pltpu.SemaphoreType.DMA((2, coarse)),
            pltpu.SemaphoreType.DMA((fine + coarse,)),
            pltpu.SemaphoreType.DMA((2,)),
            pltpu.SemaphoreType.DMA((2,)),
        ],
        compiler_params=pltpu.CompilerParams(
            collective_id=0, has_side_effects=True, vmem_limit_bytes=40 * 2**20
        ),
    )(*inputs)


def solution(mesh):
    placed = P(("clip", "blk"), None)
    return jax.shard_map(
        per_device, mesh=mesh, in_specs=(placed,) * 4, out_specs=placed, check_vma=False
    )
```
